256 devices in a mesh: gx: 128 (over y_hi, x, z, core), gy: 2 (over y_lo).
Axes of the slice: x: 4, y: 4 (y_hi: 2, y_lo: 2; y = y_hi * 2 + y_lo), z: 8, core: 2. Of those that a mesh axis runs over, the one named last changes fastest.
Arguments:
- orbitals: float32 [2, 32, 8192, 256], P(None, None, 'gx', 'gy'), may hold values from -12 to 12
- potential: float32 [32, 8192, 256], P(None, 'gx', 'gy'), may hold values from 0.5 to 2
- shift_ratio: float32 [1], replicated, may hold values from 16 to 48
Outputs:
- orbitals_next: float32 [2, 32, 8192, 256], P(None, None, 'gx', 'gy')
The draws below stay inside these ranges and needn't reach their ends.
All inputs are finite; a program needn't handle non-finite values.
Results may differ from the reference program's by a relative error of at most 0.0003.
Values sent between devices are 32-bit elements; how exact they have to be, the bound alone decides.
No kernel may reach another device: no remote copies, remote signals or barrier semaphores. Data moves between devices by JAX's collectives and lax.ppermute only.
A program may use at most 128 MiB of HBM per device.

```python
import math
import jax
import jax.numpy as jnp
from jax import lax

COMPS = 2
NX = 8192
NY = 256
NZ = 32


def draw_orbitals(key, part):
    first, second, third, fourth, fifth, sixth, seventh = jax.random.split(key, 7)
    position = jnp.arange(NX, dtype=jnp.float32) / NX
    row_scale = jnp.exp(math.log(3.0) * position + jax.random.uniform(second, (NX,), jnp.float32, -1.2, 0.0))
    column_scale = jnp.exp(jax.random.uniform(third, (NZ, 1, NY), jnp.float32, -1.2, 0.0))
    wave_mode = jax.random.randint(fourth, (COMPS, NZ, 1, 1), 37, 41).astype(jnp.float32)
    wave_phase = jax.random.uniform(fifth, (COMPS, NZ, 1, 1), jnp.float32, -math.pi, math.pi)
    wave_sign = (2 * jax.random.randint(sixth, (COMPS, NZ, 1, NY), 0, 2) - 1).astype(jnp.float32)
    wave_size = jax.random.uniform(seventh, (COMPS, NZ, 1, NY), jnp.float32, 0.5, 1.2)
    wave = 1.6 * wave_sign * wave_size * jnp.cos(2.0 * math.pi * wave_mode * position[None, None, :, None] + wave_phase)
    base = jnp.clip(jax.random.normal(first, (COMPS, NZ, NX, NY), jnp.float32), -2.0, 2.0)
    return ((base * column_scale[None] + wave) * row_scale[None, None, :, None]).astype(jnp.float32)


def block_levels(key, dims, pieces, least, top_value):
    def one(dim, blocks):
        steps = jax.random.uniform(jax.random.fold_in(jax.random.fold_in(key, 6), dim), (blocks,), jnp.float32, least / len(pieces), top_value / len(pieces))
        return jnp.repeat(jnp.exp(steps), dims[dim] // blocks).reshape((-1,) + (1,) * (len(dims) - dim - 1))

    factor_of = one(*pieces[0])
    for cut in pieces[1:]:
        factor_of = factor_of * one(*cut)
    return factor_of


def setup_inputs(seed: int = 0) -> dict:
    splits = jax.random.split(jax.random.key(seed), 4)
    orbitals = draw_orbitals(jax.random.fold_in(splits[3], 71), 0)
    potential = jnp.clip(0.5 + 1.5 * jax.random.uniform(splits[1], (NZ, NX, NY), jnp.float32) ** block_levels(splits[1], (NZ, NX, NY), ((1, 128), (2, 2)), -0.2, 0.2), 0.5, 2.0)
    shift_ratio = jnp.clip(jnp.exp(jax.random.uniform(splits[2], (1,), jnp.float32, math.log(16.0), math.log(48.0))), 16.0, 48.0)
    return dict(orbitals=orbitals, potential=potential, shift_ratio=shift_ratio)


def reference(orbitals, potential, shift_ratio):
    neighbours = jnp.roll(orbitals, 1, axis=2) + jnp.roll(orbitals, -1, axis=2)
    neighbours = neighbours + jnp.roll(orbitals, 1, axis=3) + jnp.roll(orbitals, -1, axis=3)
    neighbours = neighbours + jnp.roll(orbitals, 1, axis=1) + jnp.roll(orbitals, -1, axis=1)
    laplace = neighbours - 6.0 * orbitals
    squares = orbitals * orbitals
    density = jnp.stack([0.06 * squares[0] + 0.04 * squares[1], 0.04 * squares[0] + 0.05 * squares[1]])
    applied = -0.5 * laplace + (potential[None] + density) * orbitals
    mean_square = lax.optimization_barrier(jnp.mean(squares, axis=(1, 2, 3)))
    energy = lax.optimization_barrier(jnp.mean(orbitals * applied, axis=(1, 2, 3))) / (mean_square + 1e-06)
    residual = applied - energy[:, None, None, None] * orbitals
    sigma = shift_ratio[0] / float(NX * NX)
    freq = jnp.arange(NX).astype(residual.dtype)
    denom = sigma + 2.0 * jnp.sin(jnp.pi * freq / NX) ** 2
    gain = sigma / denom
    flat = residual.reshape(COMPS * NZ, NX, NY)

    def solve_plane(plane):
        spectrum = jnp.fft.fft(plane, axis=0)
        return jnp.real(jnp.fft.ifft(spectrum * gain[:, None], axis=0)).astype(plane.dtype)
    direction = lax.map(solve_plane, flat).reshape(residual.shape)
    update = orbitals - 4.0 * direction
    mean_update = lax.optimization_barrier(jnp.mean(update * update, axis=(1, 2, 3)))
    ratio = jnp.sqrt(mean_square / (mean_update + 1e-06))
    return update * ratio[:, None, None, None]
```

```python
import jax
import jax.numpy as jnp
from jax import lax
from jax.experimental import pallas as pl
from jax.experimental.pallas import tpu as pltpu
from jax.sharding import Mesh
from jax.sharding import PartitionSpec as P

GX = ("gx_0", "gx_1", "gx_2", "gx_3")
ALL = ("gx_0", "gx_1", "gx_2", "gx_3", "gy")

TAU = 4.0
EPS = 1e-06
COUPLING_FIRST = 0.06
COUPLING_SECOND = 0.05
COUPLING_CROSS = 0.04
HIGHEST = lax.Precision.HIGHEST

COMPS = 2
NZ = 32
NX = 64
NY = 128
LINES = COMPS * NZ
BLOCKS = 4
WIDE = NY // BLOCKS

VMEM = pl.BlockSpec(memory_space=pltpu.VMEM)
SMEM = pl.BlockSpec(memory_space=pltpu.SMEM)


def lane_of(shape):
    return lax.broadcasted_iota(jnp.int32, shape, 1)


def row_of(shape):
    return lax.broadcasted_iota(jnp.int32, shape, 0)


def plane(ref, comp, x):
    return ref[pl.ds(comp * NZ * NX + x, NZ, stride=NX), :]


def rows(x, comp):
    return pl.ds(pl.multiple_of(x * LINES + comp * NZ, NZ), NZ)


def extract_kernel(o_ref, edge_ref, first_ref, last_ref):
    lane = lane_of((NZ, NY))
    for comp in range(COMPS):
        def step(x, packed):
            rolled = pltpu.roll(plane(o_ref, comp, x), 2 * x + 1, 1)
            return jnp.where(lane // 2 == x, rolled, packed)

        packed = lax.fori_loop(0, NX, step, jnp.zeros((NZ, NY), jnp.float32), unroll=8)
        edge_ref[comp * NZ : (comp + 1) * NZ, :] = packed
        first_ref[comp * NZ : (comp + 1) * NZ, :] = plane(o_ref, comp, 0)
        last_ref[comp * NZ : (comp + 1) * NZ, :] = plane(o_ref, comp, NX - 1)


def sweep_kernel(rate_ref, gain_ref, sigma_ref, o_ref, v_ref, p_ref, q_ref, tips_ref, sums_ref, a_scr, fo_scr, fa_scr, tab_scr):
    rate = rate_ref[0]
    gain4 = TAU * gain_ref[0]
    keep = 1.0 - TAU * sigma_ref[0]
    decay = jnp.exp(jnp.full((NZ, NY), -rate, jnp.float32))
    index = row_of((NX, NY)).astype(jnp.float32)
    tab_scr[0] = jnp.exp(-rate * (index + 1.0))
    tab_scr[1] = jnp.exp(-rate * (float(NX) - index))
    zero = jnp.zeros((NZ, NY), jnp.float32)

    def ahead(x, carry):
        prev, fo, fa, cross, square = carry
        o = [plane(o_ref, c, x) for c in range(COMPS)]
        s0, s1 = o[0] * o[0], o[1] * o[1]
        base = v_ref[pl.ds(x, NZ, stride=NX), :] + 2.0
        density = [
            COUPLING_FIRST * s0 + COUPLING_CROSS * s1,
            COUPLING_CROSS * s0 + COUPLING_SECOND * s1,
        ]
        new_fo, new_fa, new_cross = [], [], []
        for c in range(COMPS):
            around = pltpu.roll(o[c], 1, 0) + pltpu.roll(o[c], NZ - 1, 0)
            left = jnp.where(lane == 0, 0.0, pltpu.roll(o[c], 1, 1))
            right = jnp.where(lane == NY - 1, 0.0, pltpu.roll(o[c], NY - 1, 1))
            a = (base + density[c]) * o[c] - 0.5 * (around + (left + right))
            new_cross.append(cross[c] + o[c] * ((a + o[c]) - prev[c]))
            f_o = decay * fo[c] + o[c]
            f_a = decay * fa[c] + a
            a_scr[rows(x, c), :] = a
            fo_scr[rows(x, c), :] = f_o
            fa_scr[rows(x, c), :] = f_a
            new_fo.append(f_o)
            new_fa.append(f_a)
        return (o, new_fo, new_fa, new_cross, [square[0] + s0, square[1] + s1])

    lane = lane_of((NZ, NY))
    two = [zero, zero]
    _, fo, fa, cross, square = lax.fori_loop(0, NX, ahead, (two, two, two, two, two), unroll=2)
    for c in range(COMPS):
        tips_ref[0, c * NZ : (c + 1) * NZ, :] = fo[c]
        tips_ref[2, c * NZ : (c + 1) * NZ, :] = fa[c]
        sums_ref[c : c + 1, :] = jnp.sum(cross[c], axis=0, keepdims=True)
        sums_ref[COMPS + c : COMPS + c + 1, :] = jnp.sum(square[c], axis=0, keepdims=True)

    for c in range(COMPS):
        def behind(k, carry):
            x = NX - 1 - k
            bo, ba, rq, sq, rp, sp = carry
            o, a = plane(o_ref, c, x), a_scr[rows(x, c), :]
            do, da = decay * bo, decay * ba
            q = gain4 * (fo_scr[rows(x, c), :] + do)
            p = keep * o - gain4 * (fa_scr[rows(x, c), :] + da)
            q_ref[rows(x, c), :] = q
            p_ref[rows(x, c), :] = p
            rise = tab_scr[0, pl.ds(x, 1), :]
            fall = tab_scr[1, pl.ds(x, 1), :]
            return (do + o, da + a, rq + rise * q, sq + fall * q, rp + rise * p, sp + fall * p)

        bo, ba, rq, sq, rp, sp = lax.fori_loop(0, NX, behind, (zero,) * 6, unroll=4)
        block = slice(c * NZ, (c + 1) * NZ)
        tips_ref[1, block, :] = bo
        tips_ref[3, block, :] = ba
        tips_ref[4, block, :] = rq
        tips_ref[5, block, :] = sq
        tips_ref[6, block, :] = rp
        tips_ref[7, block, :] = sp


def pair_matrix(weight, source):
    shape = (NY, NY)
    lane, parity = lane_of(shape), row_of(shape) % 2
    hit = ((lane == 0) & (parity == 0)) | ((lane == NY - 1) & (parity == 1))
    return jnp.where(hit, weight, 0.0)


def dot(a, b):
    return jnp.dot(a, b, precision=HIGHEST, preferred_element_type=jnp.float32)


def pack_kernel(rate_ref, gain_ref, tips_ref, sums_ref, edge_ref, halo_ref, first_ref, before_ref, msg_ref, edge_q_ref):
    rate = rate_ref[0]
    gain4 = TAU * gain_ref[0]
    halo = halo_ref[...]
    shape = (NY, NY)
    place = (row_of(shape) // 2).astype(jnp.float32)
    target = (lane_of(shape) // 2).astype(jnp.float32)
    near = jnp.exp(-rate * jnp.abs(place - target))
    swap = (row_of(shape) % 2) != (lane_of(shape) % 2)
    edge_q = gain4 * dot(halo, jnp.where(swap, near, 0.0))
    edge_q_ref[...] = edge_q
    rise = jnp.exp(-rate * (place + 1.0))
    fall = jnp.exp(-rate * (float(NX) - place))
    tip_f = jnp.exp(-rate * (float(NX - 1) - place))
    tip_b = jnp.exp(-rate * place)
    same = ((row_of(shape) % 2) == 1) & (lane_of(shape) == 0)
    same = same | (((row_of(shape) % 2) == 0) & (lane_of(shape) == NY - 1))
    tips = [tips_ref[k] for k in range(8)]
    tips[2] = tips[2] - 0.5 * dot(halo, pair_matrix(tip_f, None))
    tips[3] = tips[3] - 0.5 * dot(halo, pair_matrix(tip_b, None))
    tips[6] = tips[6] + 0.5 * dot(edge_q, jnp.where(same, rise, 0.0))
    tips[7] = tips[7] + 0.5 * dot(edge_q, jnp.where(same, fall, 0.0))

    lane = lane_of((LINES, NY))
    even = lane % 2 == 0
    swapped = jnp.where(even, pltpu.roll(halo, NY - 1, 1), pltpu.roll(halo, 1, 1))
    extra = -0.5 * (edge_ref[...] * swapped) - first_ref[...] * before_ref[...]
    row_lane = lane_of((1, NY))
    scalars = jnp.zeros((1, NY), jnp.float32)
    for c in range(COMPS):
        cross = sums_ref[c : c + 1, :] + jnp.sum(extra[c * NZ : (c + 1) * NZ, :], axis=0, keepdims=True)
        scalars = jnp.where(row_lane == c, jnp.sum(cross, axis=1, keepdims=True), scalars)
        square = jnp.sum(sums_ref[COMPS + c : COMPS + c + 1, :], axis=1, keepdims=True)
        scalars = jnp.where(row_lane == COMPS + c, square, scalars)
    everyone = jnp.broadcast_to(scalars, (LINES, NY))

    slot = lane // WIDE
    for j in range(BLOCKS):
        for g in range(2):
            line = None
            for k in range(4):
                shift = (WIDE * (k - j)) % NY
                piece = tips[4 * g + k]
                piece = pltpu.roll(piece, shift, 1) if shift else piece
                line = piece if line is None else jnp.where(slot == k, piece, line)
            msg_ref[pl.ds(3 * LINES * j + g, LINES, stride=3), :] = line
        msg_ref[pl.ds(3 * LINES * j + 2, LINES, stride=3), :] = everyone


def pick(vector, k):
    return jnp.sum(jnp.where(lane_of((1, NY)) == k, vector, 0.0), axis=1, keepdims=True)


def owner_kernel(groups, cells, me_ref, rate_ref, gain_ref, sigma_ref, got_ref, edge_q_ref, p_ref, q_ref, w_ref, back_ref, mass_ref):
    rate, gain, sigma = rate_ref[0], gain_ref[0], sigma_ref[0]
    devices = 2 * groups
    total = jnp.sum(got_ref[pl.ds(2, devices, stride=3), :], axis=0, keepdims=True)
    shifts = []
    lane1 = lane_of((1, NY))
    mass = jnp.zeros((1, NY), jnp.float32)
    for c in range(COMPS):
        mean_square = pick(total, COMPS + c) / cells
        energy = (pick(total, c) / cells) / (mean_square + EPS)
        shifts.append(energy + sigma)
        mass = jnp.where(lane1 == c, mean_square, mass)
    mass_ref[...] = jnp.broadcast_to(mass, (8, NY))

    lane = lane_of((NZ, NY))
    ends = (lane == 0) | (lane == NY - 1)
    own = []
    for c in range(COMPS):
        half = 0.5 * edge_q_ref[c * NZ : (c + 1) * NZ, :]
        shift = jnp.broadcast_to(shifts[c], (NZ, NY))

        def step(x, acc):
            edge = jnp.where(ends, pltpu.roll(half, NY - (2 * x + 1), 1), 0.0)
            w = (p_ref[rows(x, c), :] + edge) + shift * q_ref[rows(x, c), :]
            w_ref[rows(x, c), :] = w
            return acc + w * w

        acc = lax.fori_loop(0, NX, step, jnp.zeros((NZ, NY), jnp.float32), unroll=8)
        own.append(jnp.sum(jnp.sum(acc, axis=0, keepdims=True), axis=1, keepdims=True))

    comp = (me_ref[0] % LINES) // NZ
    shift = jnp.where(comp == 0, shifts[0], shifts[1])
    shape = (groups, groups)
    here, other = row_of(shape), lane_of(shape)
    block_rate = rate * float(NX)
    wrap = 1.0 - jnp.exp(jnp.full(shape, -rate * float(NX * groups), jnp.float32))
    ahead = lax.rem(here - other + (groups - 1), groups).astype(jnp.float32)
    behind = lax.rem(other - here + (groups - 1), groups).astype(jnp.float32)
    weight_f = jnp.exp(-block_rate * ahead) / wrap
    weight_b = jnp.exp(-block_rate * behind) / wrap
    wide = lane_of((groups, NY))
    upper = wide >= 2 * WIDE
    powers = jnp.exp(-2.0 * rate * (lane1 + 1).astype(jnp.float32))
    rho = jnp.sum(jnp.where(lane1 < NX, powers, 0.0), axis=1, keepdims=True)
    omega = float(NX) * jnp.exp(jnp.full((1, 1), -rate * float(NX + 1), jnp.float32))
    gain4 = TAU * gain
    part = jnp.zeros((groups, NY), jnp.float32)
    combined = []
    for y in range(2):
        tips = got_ref[pl.ds(3 * y, groups, stride=6), :]
        moments = got_ref[pl.ds(3 * y + 1, groups, stride=6), :]
        carry = jnp.where((wide // WIDE) % 2 == 0, dot(weight_f, tips), dot(weight_b, tips))
        carry = gain4 * (carry - shift * pltpu.roll(carry, 2 * WIDE, 1))
        moments = moments + shift * pltpu.roll(moments, 2 * WIDE, 1)
        mixed = jnp.where((wide // WIDE) % 2 == 0, pltpu.roll(carry, NY - WIDE, 1), pltpu.roll(carry, WIDE, 1))
        term = carry * (rho * carry + omega * mixed - 2.0 * moments)
        part = part + jnp.where(upper, term, 0.0)
        combined.append(carry)
    joined = jnp.sum(jnp.sum(part, axis=0, keepdims=True), axis=1, keepdims=True)
    scalars = jnp.zeros((1, NY), jnp.float32)
    for c in range(COMPS):
        value = own[c] + jnp.where(comp == c, joined, 0.0)
        scalars = jnp.where(lane1 == c, value, scalars)
    for y in range(2):
        back_ref[pl.ds(y, groups, stride=2), :] = jnp.where(upper, combined[y], scalars)


def finish_kernel(cells, rate_ref, got_ref, mass_ref, w_ref, out_ref, tab_scr):
    rate = rate_ref[0]
    index = row_of((NX, NY)).astype(jnp.float32)
    tab_scr[0] = jnp.exp(-rate * (index + 1.0))
    tab_scr[1] = jnp.exp(-rate * (float(NX) - index))
    total = jnp.sum(got_ref[...], axis=0, keepdims=True)
    slot = lane_of((NZ, NY)) // WIDE
    for c in range(COMPS):
        mean_square = pick(mass_ref[0:1, :], c)
        ratio = jnp.sqrt(mean_square / (pick(total, c) / cells + EPS))
        ratio = jnp.broadcast_to(ratio, (NZ, NY))
        forward = jnp.zeros((NZ, NY), jnp.float32)
        backward = jnp.zeros((NZ, NY), jnp.float32)
        for j in range(BLOCKS):
            piece = got_ref[j * LINES + c * NZ : j * LINES + (c + 1) * NZ, :]
            forward = jnp.where(slot == j, pltpu.roll(piece, (WIDE * (j - 2)) % NY, 1) if j != 2 else piece, forward)
            backward = jnp.where(slot == j, pltpu.roll(piece, (WIDE * (j - 3)) % NY, 1) if j != 3 else piece, backward)
        forward = ratio * forward
        backward = ratio * backward

        def step(x, _):
            rise = tab_scr[0, pl.ds(x, 1), :]
            fall = tab_scr[1, pl.ds(x, 1), :]
            value = ratio * w_ref[rows(x, c), :] - (rise * forward + fall * backward)
            out_ref[pl.ds(c * NZ * NX + x, NZ, stride=NX), :] = value
            return 0

        lax.fori_loop(0, NX, step, 0, unroll=8)


def f32(*shape):
    return jax.ShapeDtypeStruct(shape, jnp.float32)


def shards(orbitals, potential, shift_ratio):
    groups = lax.axis_size(GX)
    devices = lax.axis_size(ALL)
    cells = float(NZ * NX * NY * devices)
    line_cells = NX * groups
    sigma = shift_ratio / float(line_cells * line_cells)
    rate = jnp.log1p(sigma + jnp.sqrt(sigma * (sigma + 2.0)))
    gain = jnp.sqrt(sigma / (sigma + 2.0))
    me = lax.axis_index(ALL).astype(jnp.int32).reshape(1)
    o = orbitals.reshape(LINES * NX, NY)
    v = potential.reshape(NZ * NX, NY)
    cells_all = LINES * NX

    edge, first, last = pl.pallas_call(
        extract_kernel,
        out_shape=(f32(LINES, NY),) * 3,
        in_specs=[VMEM],
        out_specs=(VMEM,) * 3,
        name="extract",
    )(o)
    halo = lax.ppermute(edge, "gy", [(0, 1), (1, 0)])
    before = lax.ppermute(last, GX, [(i, (i + 1) % groups) for i in range(groups)])

    big = pltpu.VMEM((cells_all, NY), jnp.float32)
    p, q, tips, sums = pl.pallas_call(
        sweep_kernel,
        out_shape=(f32(cells_all, NY), f32(cells_all, NY), f32(8, LINES, NY), f32(2 * COMPS, NY)),
        in_specs=[SMEM, SMEM, SMEM, VMEM, VMEM],
        out_specs=(VMEM,) * 4,
        scratch_shapes=[big, big, big, pltpu.VMEM((2, NX, NY), jnp.float32)],
        name="sweep",
    )(rate, gain, sigma, o, v)

    msg, edge_q = pl.pallas_call(
        pack_kernel,
        out_shape=(f32(3 * devices, NY), f32(LINES, NY)),
        in_specs=[SMEM, SMEM] + [VMEM] * 6,
        out_specs=(VMEM,) * 2,
        name="pack",
    )(rate, gain, tips, sums, edge, halo, first, before)
    got = lax.all_to_all(msg.reshape(devices, 1, 3 * NY), ALL, 0, 0, tiled=True).reshape(3 * devices, NY)

    w, back, mass = pl.pallas_call(
        lambda *refs: owner_kernel(groups, cells, *refs),
        out_shape=(f32(cells_all, NY), f32(devices, NY), f32(8, NY)),
        in_specs=[SMEM] * 4 + [VMEM] * 4,
        out_specs=(VMEM,) * 3,
        name="owner",
    )(me, rate, gain, sigma, got, edge_q, p, q)
    returned = lax.all_to_all(back.reshape(devices, 1, NY), ALL, 0, 0, tiled=True).reshape(devices, NY)

    out = pl.pallas_call(
        lambda *refs: finish_kernel(cells, *refs),
        out_shape=f32(cells_all, NY),
        in_specs=[SMEM] + [VMEM] * 3,
        out_specs=VMEM,
        scratch_shapes=[pltpu.VMEM((2, NX, NY), jnp.float32)],
        name="finish",
    )(rate, returned, mass, w)
    return out.reshape(orbitals.shape)


def solution(mesh):
    split = Mesh(mesh.devices.reshape(2, 4, 8, 2, mesh.shape["gy"]), ALL)
    return jax.shard_map(
        shards,
        mesh=split,
        in_specs=(P(None, None, GX, "gy"), P(None, GX, "gy"), P()),
        out_specs=P(None, None, GX, "gy"),
        check_vma=False,
    )
```

```python
import jax
import jax.numpy as jnp
from jax import lax
from jax.experimental import pallas as pl
from jax.experimental.pallas import tpu as pltpu
from jax.sharding import Mesh
from jax.sharding import PartitionSpec as P

GX = ("gx_0", "gx_1", "gx_2", "gx_3")
ALL = ("gx_0", "gx_1", "gx_2", "gx_3", "gy")

TAU = 4.0
EPS = 1e-06
COUPLING_FIRST = 0.06
COUPLING_SECOND = 0.05
COUPLING_CROSS = 0.04
HIGHEST = lax.Precision.HIGHEST

COMPS = 2
NZ = 32
NX = 64
NY = 128
LINES = COMPS * NZ
BLOCKS = 4
WIDE = NY // BLOCKS
CHUNKS = 8

PARAMS = pltpu.CompilerParams(vmem_limit_bytes=16 << 20)
VMEM = pl.BlockSpec(memory_space=pltpu.VMEM)
HBM = pl.BlockSpec(memory_space=pltpu.HBM)
SMEM = pl.BlockSpec(memory_space=pltpu.SMEM)


def lane_of(shape):
    return lax.broadcasted_iota(jnp.int32, shape, 1)


def row_of(shape):
    return lax.broadcasted_iota(jnp.int32, shape, 0)


def rows(x, comp):
    return pl.ds(pl.multiple_of(x * LINES + comp * NZ, NZ), NZ)


def part(comp):
    return slice(comp * NZ, (comp + 1) * NZ)


def start_lines(source, target, sems):
    size = source.shape[0]

    def copy(x):
        place = pl.ds(pl.multiple_of(x * size, size), size)
        return pltpu.make_async_copy(source.at[:, x, :], target.at[place, :], sems.at[x])

    def start(x, _):
        copy(x).start()
        return 0

    lax.fori_loop(0, NX, start, 0, unroll=8)
    return copy


def load_kernel(o_hbm, o_ref, edge_ref, first_ref, last_ref, sems):
    copy = start_lines(o_hbm, o_ref, sems)
    lane = lane_of((NZ, NY)) // 2

    def step(x, packed):
        copy(x).wait()
        return [
            jnp.where(lane == x, pltpu.roll(o_ref[rows(x, c), :], 2 * x + 1, 1), packed[c])
            for c in range(COMPS)
        ]

    zero = jnp.zeros((NZ, NY), jnp.float32)
    packed = lax.fori_loop(0, NX, step, [zero, zero], unroll=8)
    for c in range(COMPS):
        edge_ref[part(c), :] = packed[c]
    first_ref[...] = o_ref[0:LINES, :]
    last_ref[...] = o_ref[(NX - 1) * LINES : NX * LINES, :]


def tables(rate, count):
    place = (row_of((count * NX, NY)) // count).astype(jnp.float32)
    index = row_of((NX, NY)).astype(jnp.float32)
    rise = jnp.exp(-rate * (index + 1.0))
    fall = jnp.exp(-rate * (float(NX) - index))
    shape = (count * NX, NX)
    gap = (row_of(shape) // count - lane_of(shape)).astype(jnp.float32)
    near = jnp.exp(-rate * jnp.abs(gap))
    return (
        jnp.exp(-rate * (float(NX - 1) - place)),
        jnp.exp(-rate * place),
        dot(near, rise),
        dot(near, fall),
    )


def gather_kernel(rate_ref, gain_ref, sigma_ref, o_ref, v_hbm, a_ref, tips_ref, sums_ref, v_scr, tab_scr, sems):
    copy = start_lines(v_hbm, v_scr, sems)
    rate = rate_ref[0]
    gain4 = TAU * gain_ref[0]
    keep = 1.0 - TAU * sigma_ref[0]
    for k, table in enumerate(tables(rate, 1)):
        tab_scr[k] = table
    zero = jnp.zeros((NZ, NY), jnp.float32)
    decay = jnp.exp(jnp.full((NZ, NY), -rate, jnp.float32))

    def step(x, carry):
        cross, square, sums = carry
        copy(x).wait()
        o = [o_ref[rows(x, c), :] for c in range(COMPS)]
        back = jnp.maximum(x - 1, 0)
        real = jnp.where(x > 0, 1.0, 0.0)
        weights = [tab_scr[k, pl.ds(x, 1), :] for k in range(4)]
        s = [o[0] * o[0], o[1] * o[1]]
        both = COUPLING_CROSS * (s[0] + s[1])
        base = (v_scr[pl.ds(pl.multiple_of(x * NZ, NZ), NZ), :] + 2.0) + both
        own = (COUPLING_FIRST - COUPLING_CROSS, COUPLING_SECOND - COUPLING_CROSS)
        new_cross, new_square, new_sums = [], [], []
        for c in range(COMPS):
            around = pltpu.roll(o[c], 1, 0) + pltpu.roll(o[c], NZ - 1, 0)
            around = around + (pltpu.roll(o[c], 1, 1) + pltpu.roll(o[c], NY - 1, 1))
            a = (base + own[c] * s[c]) * o[c] - 0.5 * around
            a_ref[rows(x, c), :] = a
            prev = real * o_ref[rows(back, c), :]
            new_cross.append(cross[c] + o[c] * ((a + o[c]) - prev))
            new_square.append(square[c] + s[c])
            new_sums.append(
                [decay * sums[c][0] + o[c], decay * sums[c][1] + a]
                + [sums[c][1 + k] + weights[k] * o[c] for k in range(1, 4)]
                + [sums[c][4 + k] + weights[k] * a for k in range(1, 4)]
            )
        return new_cross, new_square, new_sums

    cross, square, sums = lax.fori_loop(
        0, NX, step, ([zero] * 2, [zero] * 2, [[zero] * 8] * 2), unroll=2
    )
    once = jnp.exp(jnp.full((NZ, NY), -rate, jnp.float32))
    for c in range(COMPS):
        f_o, f_a, b_o, r_o, s_o, b_a, r_a, s_a = sums[c]
        tips_ref[0, part(c), :] = f_o
        tips_ref[1, part(c), :] = b_o
        tips_ref[2, part(c), :] = f_a
        tips_ref[3, part(c), :] = b_a
        tips_ref[4, part(c), :] = gain4 * r_o
        tips_ref[5, part(c), :] = gain4 * s_o
        tips_ref[6, part(c), :] = keep * (once * b_o) - gain4 * r_a
        tips_ref[7, part(c), :] = keep * (once * f_o) - gain4 * s_a
        sums_ref[c : c + 1, :] = jnp.sum(cross[c], axis=0, keepdims=True)
        sums_ref[COMPS + c : COMPS + c + 1, :] = jnp.sum(square[c], axis=0, keepdims=True)


def local_shift(sums_ref, c, sigma):
    cross = jnp.sum(sums_ref[c : c + 1, :], axis=1, keepdims=True)
    square = jnp.sum(sums_ref[COMPS + c : COMPS + c + 1, :], axis=1, keepdims=True)
    return cross / (square + EPS) + sigma


def sweep_kernel(rate_ref, gain_ref, sigma_ref, o_hbm, a_ref, edge_ref, halo_ref, sums_ref, p_ref, q_ref, local_ref, o_ref, fo_scr, fa_scr, sems):
    copy = start_lines(o_hbm, o_ref, sems)
    gain4 = TAU * gain_ref[0]
    keep = 1.0 - TAU * sigma_ref[0]
    decay = jnp.exp(jnp.full((NZ, NY), -rate_ref[0], jnp.float32))
    lane = lane_of((NZ, NY))
    zero = jnp.zeros((NZ, NY), jnp.float32)
    lane1 = lane_of((1, NY))
    for c in range(COMPS):
        delta = -0.5 * (halo_ref[part(c), :] - edge_ref[part(c), :])
        even = lane % 2 == 0
        delta = jnp.where(even, pltpu.roll(delta, NY - 1, 1), pltpu.roll(delta, 1, 1))
        ends = (lane == 0) | (lane == NY - 1)

        def ahead(x, carry):
            fo, fa = carry
            if c == 0:
                copy(x).wait()
            o = o_ref[rows(x, c), :]
            a = a_ref[rows(x, c), :] + jnp.where(ends, pltpu.roll(delta, NY - (2 * x + 1), 1), 0.0)
            fo = decay * fo + o
            fa = decay * fa + a
            fo_scr[pl.ds(pl.multiple_of(x * NZ, NZ), NZ), :] = fo
            fa_scr[pl.ds(pl.multiple_of(x * NZ, NZ), NZ), :] = fa
            p_ref[rows(x, c), :] = a
            return fo, fa

        lax.fori_loop(0, NX, ahead, (zero, zero), unroll=4)
        shift = jnp.broadcast_to(local_shift(sums_ref, c, sigma_ref[0]), (NZ, NY))

        def behind(k, carry):
            x = NX - 1 - k
            bo, ba, ww, wq, qq = carry
            o, a = o_ref[rows(x, c), :], p_ref[rows(x, c), :]
            do, da = decay * bo, decay * ba
            q = gain4 * (fo_scr[pl.ds(pl.multiple_of(x * NZ, NZ), NZ), :] + do)
            p = keep * o - gain4 * (fa_scr[pl.ds(pl.multiple_of(x * NZ, NZ), NZ), :] + da)
            q_ref[rows(x, c), :] = q
            p_ref[rows(x, c), :] = p
            w = p + shift * q
            return do + o, da + a, ww + w * w, wq + w * q, qq + q * q

        _, _, ww, wq, qq = lax.fori_loop(0, NX, behind, (zero,) * 5, unroll=4)
        for k, value in enumerate((ww, wq, qq)):
            local_ref[3 * c + k : 3 * c + k + 1, :] = jnp.sum(value, axis=0, keepdims=True)


def dot(a, b):
    return jnp.dot(a, b, precision=HIGHEST, preferred_element_type=jnp.float32)


def pack_kernel(rate_ref, gain_ref, tips_ref, sums_ref, edge_ref, halo_ref, first_ref, before_ref, msg_ref):
    gain4 = TAU * gain_ref[0]
    halo = halo_ref[...]
    delta = -0.5 * (halo - edge_ref[...])
    shape = (NY, NY)
    odd = row_of(shape) % 2
    hit = ((lane_of(shape) == 0) & (odd == 0)) | ((lane_of(shape) == NY - 1) & (odd == 1))
    fixes = [dot(delta, jnp.where(hit, table, 0.0)) for table in tables(rate_ref[0], 2)]
    tips = [tips_ref[k] for k in range(8)]
    tips[2] = tips[2] + fixes[0]
    tips[3] = tips[3] + fixes[1]
    tips[6] = tips[6] - gain4 * fixes[2]
    tips[7] = tips[7] - gain4 * fixes[3]

    lane = lane_of((LINES, NY))
    even = lane % 2 == 0
    swapped = jnp.where(even, pltpu.roll(delta, NY - 1, 1), pltpu.roll(delta, 1, 1))
    extra = edge_ref[...] * swapped - first_ref[...] * before_ref[...]
    row_lane = lane_of((1, NY))
    scalars = jnp.zeros((1, NY), jnp.float32)
    for c in range(COMPS):
        cross = sums_ref[c : c + 1, :] + jnp.sum(extra[c * NZ : (c + 1) * NZ, :], axis=0, keepdims=True)
        scalars = jnp.where(row_lane == c, jnp.sum(cross, axis=1, keepdims=True), scalars)
        square = jnp.sum(sums_ref[COMPS + c : COMPS + c + 1, :], axis=1, keepdims=True)
        scalars = jnp.where(row_lane == COMPS + c, square, scalars)
    everyone = jnp.broadcast_to(scalars, (LINES, NY))

    slot = lane // WIDE
    for j in range(BLOCKS):
        for g in range(2):
            line = None
            for k in range(4):
                shift = (WIDE * (k - j)) % NY
                piece = tips[4 * g + k]
                piece = pltpu.roll(piece, shift, 1) if shift else piece
                line = piece if line is None else jnp.where(slot == k, piece, line)
            msg_ref[pl.ds(3 * LINES * j + g, LINES, stride=3), :] = line
        msg_ref[pl.ds(3 * LINES * j + 2, LINES, stride=3), :] = everyone


def pick(vector, k):
    return jnp.sum(jnp.where(lane_of((1, NY)) == k, vector, 0.0), axis=1, keepdims=True)


def owner_kernel(groups, cells, me_ref, rate_ref, gain_ref, sigma_ref, got_ref, sums_ref, local_ref, back_ref, mass_ref):
    rate, gain, sigma = rate_ref[0], gain_ref[0], sigma_ref[0]
    devices = 2 * groups
    total = jnp.sum(got_ref[pl.ds(2, devices, stride=3), :], axis=0, keepdims=True)
    shifts, own = [], []
    lane1 = lane_of((1, NY))
    mass = jnp.zeros((1, NY), jnp.float32)
    for c in range(COMPS):
        mean_square = pick(total, COMPS + c) / cells
        energy = (pick(total, c) / cells) / (mean_square + EPS)
        shift = energy + sigma
        shifts.append(shift)
        mass = jnp.where(lane1 == c, mean_square, mass)
        mass = jnp.where(lane1 == COMPS + c, shift, mass)
        ww, wq, qq = [
            jnp.sum(local_ref[3 * c + k : 3 * c + k + 1, :], axis=1, keepdims=True) for k in range(3)
        ]
        more = shift - local_shift(sums_ref, c, sigma)
        own.append(ww + more * (2.0 * wq + more * qq))
    mass_ref[...] = jnp.broadcast_to(mass, (8, NY))

    comp = (me_ref[0] % LINES) // NZ
    shift = jnp.where(comp == 0, shifts[0], shifts[1])
    shape = (groups, groups)
    here, other = row_of(shape), lane_of(shape)
    block_rate = rate * float(NX)
    wrap = 1.0 - jnp.exp(jnp.full(shape, -rate * float(NX * groups), jnp.float32))
    ahead = lax.rem(here - other + (groups - 1), groups).astype(jnp.float32)
    behind = lax.rem(other - here + (groups - 1), groups).astype(jnp.float32)
    weight_f = jnp.exp(-block_rate * ahead) / wrap
    weight_b = jnp.exp(-block_rate * behind) / wrap
    wide = lane_of((groups, NY))
    upper = wide >= 2 * WIDE
    powers = jnp.exp(-2.0 * rate * (lane1 + 1).astype(jnp.float32))
    rho = jnp.sum(jnp.where(lane1 < NX, powers, 0.0), axis=1, keepdims=True)
    omega = float(NX) * jnp.exp(jnp.full((1, 1), -rate * float(NX + 1), jnp.float32))
    gain4 = TAU * gain
    joined = jnp.zeros((groups, NY), jnp.float32)
    combined = []
    for y in range(2):
        tips = got_ref[pl.ds(3 * y, groups, stride=6), :]
        moments = got_ref[pl.ds(3 * y + 1, groups, stride=6), :]
        carry = jnp.where((wide // WIDE) % 2 == 0, dot(weight_f, tips), dot(weight_b, tips))
        carry = gain4 * (carry - shift * pltpu.roll(carry, 2 * WIDE, 1))
        moments = moments + shift * pltpu.roll(moments, 2 * WIDE, 1)
        mixed = jnp.where((wide // WIDE) % 2 == 0, pltpu.roll(carry, NY - WIDE, 1), pltpu.roll(carry, WIDE, 1))
        term = carry * (rho * carry + omega * mixed - 2.0 * moments)
        joined = joined + jnp.where(upper, term, 0.0)
        combined.append(carry)
    joined = jnp.sum(jnp.sum(joined, axis=0, keepdims=True), axis=1, keepdims=True)
    scalars = jnp.zeros((1, NY), jnp.float32)
    for c in range(COMPS):
        value = own[c] + jnp.where(comp == c, joined, 0.0)
        scalars = jnp.where(lane1 == c, value, scalars)
    for y in range(2):
        back_ref[pl.ds(y, groups, stride=2), :] = jnp.where(upper, combined[y], scalars)


def finish_kernel(cells, rate_ref, got_ref, mass_ref, p_hbm, q_hbm, out_hbm, p_ref, q_ref, out_scr, tab_scr, sems, in_sems):
    def copy(x):
        source = out_scr.at[pl.ds(pl.multiple_of(x * LINES, LINES), LINES), :]
        return pltpu.make_async_copy(source, out_hbm.at[:, x, :], sems.at[x])

    size = NX * LINES // CHUNKS

    def fetch(k):
        block = pl.ds(pl.multiple_of(k * size, size), size)
        return (
            pltpu.make_async_copy(p_hbm.at[block, :], p_ref.at[block, :], in_sems.at[0, k]),
            pltpu.make_async_copy(q_hbm.at[block, :], q_ref.at[block, :], in_sems.at[1, k]),
        )

    for k in range(CHUNKS):
        for one in fetch(k):
            one.start()
    rate = rate_ref[0]
    index = row_of((NX, NY)).astype(jnp.float32)
    tab_scr[0] = jnp.exp(-rate * (index + 1.0))
    tab_scr[1] = jnp.exp(-rate * (float(NX) - index))
    total = jnp.sum(got_ref[...], axis=0, keepdims=True)
    slot = lane_of((NZ, NY)) // WIDE
    terms = []
    for c in range(COMPS):
        mean_square = pick(mass_ref[0:1, :], c)
        ratio = jnp.sqrt(mean_square / (pick(total, c) / cells + EPS))
        lifted = jnp.broadcast_to(ratio * pick(mass_ref[0:1, :], COMPS + c), (NZ, NY))
        ratio = jnp.broadcast_to(ratio, (NZ, NY))
        forward = jnp.zeros((NZ, NY), jnp.float32)
        backward = jnp.zeros((NZ, NY), jnp.float32)
        for j in range(BLOCKS):
            piece = got_ref[j * LINES + c * NZ : j * LINES + (c + 1) * NZ, :]
            forward = jnp.where(slot == j, pltpu.roll(piece, (WIDE * (j - 2)) % NY, 1) if j != 2 else piece, forward)
            backward = jnp.where(slot == j, pltpu.roll(piece, (WIDE * (j - 3)) % NY, 1) if j != 3 else piece, backward)
        terms.append((ratio, lifted, ratio * forward, ratio * backward))

    def step(x, _):
        rise = tab_scr[0, pl.ds(x, 1), :]
        fall = tab_scr[1, pl.ds(x, 1), :]
        for c in range(COMPS):
            ratio, lifted, forward, backward = terms[c]
            value = ratio * p_ref[rows(x, c), :] + lifted * q_ref[rows(x, c), :]
            out_scr[rows(x, c), :] = value - (rise * forward + fall * backward)
        copy(x).start()
        return 0

    def drain(x, _):
        copy(x).wait()
        return 0

    def chunk(k, _):
        for one in fetch(k):
            one.wait()
        return lax.fori_loop(0, NX // CHUNKS, lambda i, z: step(k * (NX // CHUNKS) + i, z), 0, unroll=True)

    lax.fori_loop(0, CHUNKS, chunk, 0)
    lax.fori_loop(0, NX, drain, 0, unroll=8)


def far(x):
    return pltpu.with_memory_space_constraint(x, pltpu.HBM)


def near(x):
    return pltpu.with_memory_space_constraint(x, pltpu.VMEM)


def f32(*shape):
    return jax.ShapeDtypeStruct(shape, jnp.float32)


def shards(orbitals, potential, shift_ratio):
    groups = lax.axis_size(GX)
    devices = lax.axis_size(ALL)
    cells = float(NZ * NX * NY * devices)
    line_cells = NX * groups
    sigma = shift_ratio / float(line_cells * line_cells)
    rate = jnp.log1p(sigma + jnp.sqrt(sigma * (sigma + 2.0)))
    gain = jnp.sqrt(sigma / (sigma + 2.0))
    me = lax.axis_index(ALL).astype(jnp.int32).reshape(1)
    o = far(orbitals.reshape(LINES, NX, NY))
    cells_all = LINES * NX
    big = pltpu.VMEM((cells_all, NY), jnp.float32)
    row = pltpu.VMEM((LINES, NY), jnp.float32)
    small = pltpu.VMEM((8, NY), jnp.float32)
    queue = pltpu.SemaphoreType.DMA((NX,))

    o_near, edge, first, last = pl.pallas_call(
        load_kernel,
        out_shape=(big, row, row, row),
        in_specs=[HBM],
        out_specs=(VMEM,) * 4,
        scratch_shapes=[queue],
        name="load",
        compiler_params=PARAMS,
    )(o)
    halo = near(lax.ppermute(edge, "gy", [(0, 1), (1, 0)]))
    before = near(lax.ppermute(last, GX, [(i, (i + 1) % groups) for i in range(groups)]))
    o_near, edge, first = near(o_near), near(edge), near(first)

    a, tips, sums = pl.pallas_call(
        gather_kernel,
        out_shape=(big, pltpu.VMEM((8, LINES, NY), jnp.float32), small),
        in_specs=[SMEM, SMEM, SMEM, VMEM, HBM],
        out_specs=(VMEM,) * 3,
        scratch_shapes=[
            pltpu.VMEM((NX * NZ, NY), jnp.float32),
            pltpu.VMEM((4, NX, NY), jnp.float32),
            queue,
        ],
        name="gather",
        compiler_params=PARAMS,
    )(rate, gain, sigma, o_near, far(potential))
    a, tips, sums = near(a), near(tips), near(sums)

    msg = pl.pallas_call(
        pack_kernel,
        out_shape=pltpu.VMEM((3 * devices, NY), jnp.float32),
        in_specs=[SMEM, SMEM] + [VMEM] * 6,
        out_specs=VMEM,
        name="pack",
        compiler_params=PARAMS,
    )(rate, gain, tips, sums, edge, halo, first, before)
    got = lax.all_to_all(msg.reshape(devices, 1, 3 * NY), ALL, 0, 0, tiled=True).reshape(3 * devices, NY)

    p, q, local = pl.pallas_call(
        sweep_kernel,
        out_shape=(big, big, small),
        in_specs=[SMEM] * 3 + [HBM] + [VMEM] * 4,
        out_specs=(VMEM,) * 3,
        scratch_shapes=[big] + [pltpu.VMEM((NX * NZ, NY), jnp.float32)] * 2 + [queue],
        name="sweep",
        compiler_params=PARAMS,
    )(rate, gain, sigma, o, a, edge, halo, sums)
    local = near(local)

    back, mass = pl.pallas_call(
        lambda *refs: owner_kernel(groups, cells, *refs),
        out_shape=(pltpu.VMEM((devices, NY), jnp.float32), small),
        in_specs=[SMEM] * 4 + [VMEM] * 3,
        out_specs=(VMEM,) * 2,
        name="owner",
        compiler_params=PARAMS,
    )(me, rate, gain, sigma, near(got), sums, local)
    returned = lax.all_to_all(back.reshape(devices, 1, NY), ALL, 0, 0, tiled=True).reshape(devices, NY)

    out = pl.pallas_call(
        lambda *refs: finish_kernel(cells, *refs),
        out_shape=f32(LINES, NX, NY),
        in_specs=[SMEM, VMEM, VMEM, HBM, HBM],
        out_specs=HBM,
        scratch_shapes=[
            big,
            big,
            big,
            pltpu.VMEM((2, NX, NY), jnp.float32),
            queue,
            pltpu.SemaphoreType.DMA((2, CHUNKS)),
        ],
        name="finish",
        compiler_params=PARAMS,
    )(rate, near(returned), near(mass), far(p), far(q))
    return out.reshape(orbitals.shape)


def solution(mesh):
    split = Mesh(mesh.devices.reshape(2, 4, 8, 2, mesh.shape["gy"]), ALL)
    return jax.shard_map(
        shards,
        mesh=split,
        in_specs=(P(None, None, GX, "gy"), P(None, GX, "gy"), P()),
        out_specs=P(None, None, GX, "gy"),
        check_vma=False,
    )
```

```python
import jax
import jax.numpy as jnp
from jax import lax
from jax.experimental import pallas as pl
from jax.experimental.pallas import tpu as pltpu
from jax.sharding import Mesh
from jax.sharding import PartitionSpec as P

GX = ("gx_0", "gx_1", "gx_2", "gx_3")
ALL = ("gx_0", "gx_1", "gx_2", "gx_3", "gy")

TAU = 4.0
EPS = 1e-06
COUPLING_FIRST = 0.06
COUPLING_SECOND = 0.05
COUPLING_CROSS = 0.04
HIGHEST = lax.Precision.HIGHEST

COMPS = 2
NZ = 32
NX = 64
NY = 128
LINES = COMPS * NZ
BLOCKS = 4
WIDE = NY // BLOCKS
PITCH = NX + 8
ROWS = 8

PARAMS = pltpu.CompilerParams(vmem_limit_bytes=16 << 20)
VMEM = pl.BlockSpec(memory_space=pltpu.VMEM)
HBM = pl.BlockSpec(memory_space=pltpu.HBM)
SMEM = pl.BlockSpec(memory_space=pltpu.SMEM)


def lane_of(shape):
    return lax.broadcasted_iota(jnp.int32, shape, 1)


def row_of(shape):
    return lax.broadcasted_iota(jnp.int32, shape, 0)


def rows(x, comp):
    return pl.ds(pl.multiple_of(x * LINES + comp * NZ, NZ), NZ)


def part(comp):
    return slice(comp * NZ, (comp + 1) * NZ)


def start_planes(source, target, sems):
    def copy(k):
        place = pl.ds(pl.multiple_of(k * PITCH, 8), NX)
        return pltpu.make_async_copy(source.at[k], target.at[place, :], sems.at[k])

    def start(k, _):
        copy(k).start()
        return 0

    lax.fori_loop(0, source.shape[0], start, 0, unroll=8)

    def wait(first, last):
        def one(k, _):
            copy(k).wait()
            return 0

        lax.fori_loop(first, last, one, 0, unroll=8)

    return wait


def line_rows(x, comp=0):
    return pl.ds(comp * NZ * PITCH + x, NZ, stride=PITCH)


def load_kernel(o_hbm, o_ref, edge_ref, first_ref, last_ref, sems):
    wait = start_planes(o_hbm, o_ref, sems)
    lane = lane_of((NZ, NY)) // 2
    for c in range(COMPS):
        wait(c * NZ, (c + 1) * NZ)

        def step(x, packed):
            return jnp.where(lane == x, pltpu.roll(o_ref[line_rows(x, c), :], 2 * x + 1, 1), packed)

        edge_ref[part(c), :] = lax.fori_loop(0, NX, step, jnp.zeros((NZ, NY), jnp.float32), unroll=8)
        first_ref[part(c), :] = o_ref[line_rows(0, c), :]
        last_ref[part(c), :] = o_ref[line_rows(NX - 1, c), :]


def tables(rate, count):
    place = (row_of((count * NX, NY)) // count).astype(jnp.float32)
    index = row_of((NX, NY)).astype(jnp.float32)
    rise = jnp.exp(-rate * (index + 1.0))
    fall = jnp.exp(-rate * (float(NX) - index))
    shape = (count * NX, NX)
    gap = (row_of(shape) // count - lane_of(shape)).astype(jnp.float32)
    near = jnp.exp(-rate * jnp.abs(gap))
    return (
        jnp.exp(-rate * (float(NX - 1) - place)),
        jnp.exp(-rate * place),
        dot(near, rise),
        dot(near, fall),
    )


def gather_kernel(rate_ref, gain_ref, sigma_ref, o_ref, v_hbm, a_ref, tips_ref, sums_ref, v_scr, tab_scr, sems):
    wait = start_planes(v_hbm, v_scr, sems)
    rate = rate_ref[0]
    gain4 = TAU * gain_ref[0]
    keep = 1.0 - TAU * sigma_ref[0]
    for k, table in enumerate(tables(rate, 1)):
        tab_scr[k] = table
    zero = jnp.zeros((NZ, NY), jnp.float32)
    decay = jnp.exp(jnp.full((NZ, NY), -rate, jnp.float32))

    def step(x, carry):
        before, cross, square, sums = carry
        o = [o_ref[line_rows(x, c), :] for c in range(COMPS)]
        weights = [tab_scr[k, pl.ds(x, 1), :] for k in range(4)]
        s = [o[0] * o[0], o[1] * o[1]]
        both = COUPLING_CROSS * (s[0] + s[1])
        base = (v_scr[line_rows(x), :] + 2.0) + both
        own = (COUPLING_FIRST - COUPLING_CROSS, COUPLING_SECOND - COUPLING_CROSS)
        new_cross, new_square, new_sums = [], [], []
        for c in range(COMPS):
            around = pltpu.roll(o[c], 1, 0) + pltpu.roll(o[c], NZ - 1, 0)
            around = around + (pltpu.roll(o[c], 1, 1) + pltpu.roll(o[c], NY - 1, 1))
            a = (base + own[c] * s[c]) * o[c] - 0.5 * around
            a_ref[rows(x, c), :] = a
            new_cross.append(cross[c] + o[c] * ((a + o[c]) - before[c]))
            new_square.append(square[c] + s[c])
            new_sums.append(
                [decay * sums[c][0] + o[c], decay * sums[c][1] + a]
                + [sums[c][1 + k] + weights[k] * o[c] for k in range(1, 4)]
                + [sums[c][4 + k] + weights[k] * a for k in range(1, 4)]
            )
        return o, new_cross, new_square, new_sums

    wait(0, NZ)
    _, cross, square, sums = lax.fori_loop(
        0, NX, step, ([zero] * 2, [zero] * 2, [zero] * 2, [[zero] * 8] * 2), unroll=2
    )
    once = jnp.exp(jnp.full((NZ, NY), -rate, jnp.float32))
    for c in range(COMPS):
        f_o, f_a, b_o, r_o, s_o, b_a, r_a, s_a = sums[c]
        tips_ref[0, part(c), :] = f_o
        tips_ref[1, part(c), :] = b_o
        tips_ref[2, part(c), :] = f_a
        tips_ref[3, part(c), :] = b_a
        tips_ref[4, part(c), :] = gain4 * r_o
        tips_ref[5, part(c), :] = gain4 * s_o
        tips_ref[6, part(c), :] = keep * (once * b_o) - gain4 * r_a
        tips_ref[7, part(c), :] = keep * (once * f_o) - gain4 * s_a
        sums_ref[c : c + 1, :] = jnp.sum(cross[c], axis=0, keepdims=True)
        sums_ref[COMPS + c : COMPS + c + 1, :] = jnp.sum(square[c], axis=0, keepdims=True)


def local_shift(sums_ref, c, sigma):
    cross = jnp.sum(sums_ref[c : c + 1, :], axis=1, keepdims=True)
    square = jnp.sum(sums_ref[COMPS + c : COMPS + c + 1, :], axis=1, keepdims=True)
    return cross / (square + EPS) + sigma


def sweep_kernel(rate_ref, gain_ref, sigma_ref, o_hbm, a_ref, edge_ref, halo_ref, sums_ref, p_ref, q_ref, local_ref, o_ref, fo_scr, fa_scr, a_scr, sems):
    wait = start_planes(o_hbm, o_ref, sems)
    gain4 = TAU * gain_ref[0]
    keep = 1.0 - TAU * sigma_ref[0]
    decay = jnp.exp(jnp.full((NZ, NY), -rate_ref[0], jnp.float32))
    lane = lane_of((NZ, NY))
    zero = jnp.zeros((NZ, NY), jnp.float32)
    lane1 = lane_of((1, NY))
    for c in range(COMPS):
        delta = -0.5 * (halo_ref[part(c), :] - edge_ref[part(c), :])
        even = lane % 2 == 0
        delta = jnp.where(even, pltpu.roll(delta, NY - 1, 1), pltpu.roll(delta, 1, 1))
        ends = (lane == 0) | (lane == NY - 1)

        def ahead(x, carry):
            fo, fa = carry
            o = o_ref[line_rows(x, c), :]
            a = a_ref[rows(x, c), :] + jnp.where(ends, pltpu.roll(delta, NY - (2 * x + 1), 1), 0.0)
            fo = decay * fo + o
            fa = decay * fa + a
            fo_scr[pl.ds(pl.multiple_of(x * NZ, NZ), NZ), :] = fo
            fa_scr[pl.ds(pl.multiple_of(x * NZ, NZ), NZ), :] = fa
            a_scr[pl.ds(pl.multiple_of(x * NZ, NZ), NZ), :] = a
            return fo, fa

        wait(c * NZ, (c + 1) * NZ)
        lax.fori_loop(0, NX, ahead, (zero, zero), unroll=4)
        shift = jnp.broadcast_to(local_shift(sums_ref, c, sigma_ref[0]), (NZ, NY))

        def behind(k, carry):
            x = NX - 1 - k
            bo, ba, ww, wq, qq = carry
            o, a = o_ref[line_rows(x, c), :], a_scr[pl.ds(pl.multiple_of(x * NZ, NZ), NZ), :]
            do, da = decay * bo, decay * ba
            q = gain4 * (fo_scr[pl.ds(pl.multiple_of(x * NZ, NZ), NZ), :] + do)
            p = keep * o - gain4 * (fa_scr[pl.ds(pl.multiple_of(x * NZ, NZ), NZ), :] + da)
            for b in range(NZ // ROWS):
                place = pl.ds(pl.multiple_of(((c * NZ // ROWS + b) * NX + x) * ROWS, ROWS), ROWS)
                q_ref[place, :] = q[b * ROWS : (b + 1) * ROWS, :]
                p_ref[place, :] = p[b * ROWS : (b + 1) * ROWS, :]
            w = p + shift * q
            return do + o, da + a, ww + w * w, wq + w * q, qq + q * q

        _, _, ww, wq, qq = lax.fori_loop(0, NX, behind, (zero,) * 5, unroll=4)
        for k, value in enumerate((ww, wq, qq)):
            local_ref[3 * c + k : 3 * c + k + 1, :] = jnp.sum(value, axis=0, keepdims=True)


def dot(a, b):
    return jnp.dot(a, b, precision=HIGHEST, preferred_element_type=jnp.float32)


def pack_kernel(rate_ref, gain_ref, tips_ref, sums_ref, edge_ref, halo_ref, first_ref, before_ref, msg_ref):
    gain4 = TAU * gain_ref[0]
    halo = halo_ref[...]
    delta = -0.5 * (halo - edge_ref[...])
    shape = (NY, NY)
    odd = row_of(shape) % 2
    hit = ((lane_of(shape) == 0) & (odd == 0)) | ((lane_of(shape) == NY - 1) & (odd == 1))
    fixes = [dot(delta, jnp.where(hit, table, 0.0)) for table in tables(rate_ref[0], 2)]
    tips = [tips_ref[k] for k in range(8)]
    tips[2] = tips[2] + fixes[0]
    tips[3] = tips[3] + fixes[1]
    tips[6] = tips[6] - gain4 * fixes[2]
    tips[7] = tips[7] - gain4 * fixes[3]

    lane = lane_of((LINES, NY))
    even = lane % 2 == 0
    swapped = jnp.where(even, pltpu.roll(delta, NY - 1, 1), pltpu.roll(delta, 1, 1))
    extra = edge_ref[...] * swapped - first_ref[...] * before_ref[...]
    row_lane = lane_of((1, NY))
    scalars = jnp.zeros((1, NY), jnp.float32)
    for c in range(COMPS):
        cross = sums_ref[c : c + 1, :] + jnp.sum(extra[c * NZ : (c + 1) * NZ, :], axis=0, keepdims=True)
        scalars = jnp.where(row_lane == c, jnp.sum(cross, axis=1, keepdims=True), scalars)
        square = jnp.sum(sums_ref[COMPS + c : COMPS + c + 1, :], axis=1, keepdims=True)
        scalars = jnp.where(row_lane == COMPS + c, square, scalars)
    everyone = jnp.broadcast_to(scalars, (LINES, NY))

    slot = lane // WIDE
    for j in range(BLOCKS):
        for g in range(2):
            line = None
            for k in range(4):
                shift = (WIDE * (k - j)) % NY
                piece = tips[4 * g + k]
                piece = pltpu.roll(piece, shift, 1) if shift else piece
                line = piece if line is None else jnp.where(slot == k, piece, line)
            msg_ref[pl.ds(3 * LINES * j + g, LINES, stride=3), :] = line
        msg_ref[pl.ds(3 * LINES * j + 2, LINES, stride=3), :] = everyone


def pick(vector, k):
    return jnp.sum(jnp.where(lane_of((1, NY)) == k, vector, 0.0), axis=1, keepdims=True)


def owner_kernel(groups, cells, me_ref, rate_ref, gain_ref, sigma_ref, got_ref, sums_ref, local_ref, back_ref, mass_ref):
    rate, gain, sigma = rate_ref[0], gain_ref[0], sigma_ref[0]
    devices = 2 * groups
    total = jnp.sum(got_ref[pl.ds(2, devices, stride=3), :], axis=0, keepdims=True)
    shifts, own = [], []
    lane1 = lane_of((1, NY))
    mass = jnp.zeros((1, NY), jnp.float32)
    for c in range(COMPS):
        mean_square = pick(total, COMPS + c) / cells
        energy = (pick(total, c) / cells) / (mean_square + EPS)
        shift = energy + sigma
        shifts.append(shift)
        mass = jnp.where(lane1 == c, mean_square, mass)
        mass = jnp.where(lane1 == COMPS + c, shift, mass)
        ww, wq, qq = [
            jnp.sum(local_ref[3 * c + k : 3 * c + k + 1, :], axis=1, keepdims=True) for k in range(3)
        ]
        more = shift - local_shift(sums_ref, c, sigma)
        own.append(ww + more * (2.0 * wq + more * qq))
    mass_ref[...] = jnp.broadcast_to(mass, (8, NY))

    comp = (me_ref[0] % LINES) // NZ
    shift = jnp.where(comp == 0, shifts[0], shifts[1])
    shape = (groups, groups)
    here, other = row_of(shape), lane_of(shape)
    block_rate = rate * float(NX)
    wrap = 1.0 - jnp.exp(jnp.full(shape, -rate * float(NX * groups), jnp.float32))
    ahead = lax.rem(here - other + (groups - 1), groups).astype(jnp.float32)
    behind = lax.rem(other - here + (groups - 1), groups).astype(jnp.float32)
    weight_f = jnp.exp(-block_rate * ahead) / wrap
    weight_b = jnp.exp(-block_rate * behind) / wrap
    wide = lane_of((groups, NY))
    upper = wide >= 2 * WIDE
    powers = jnp.exp(-2.0 * rate * (lane1 + 1).astype(jnp.float32))
    rho = jnp.sum(jnp.where(lane1 < NX, powers, 0.0), axis=1, keepdims=True)
    omega = float(NX) * jnp.exp(jnp.full((1, 1), -rate * float(NX + 1), jnp.float32))
    gain4 = TAU * gain
    joined = jnp.zeros((groups, NY), jnp.float32)
    combined = []
    for y in range(2):
        tips = got_ref[pl.ds(3 * y, groups, stride=6), :]
        moments = got_ref[pl.ds(3 * y + 1, groups, stride=6), :]
        carry = jnp.where((wide // WIDE) % 2 == 0, dot(weight_f, tips), dot(weight_b, tips))
        carry = gain4 * (carry - shift * pltpu.roll(carry, 2 * WIDE, 1))
        moments = moments + shift * pltpu.roll(moments, 2 * WIDE, 1)
        mixed = jnp.where((wide // WIDE) % 2 == 0, pltpu.roll(carry, NY - WIDE, 1), pltpu.roll(carry, WIDE, 1))
        term = carry * (rho * carry + omega * mixed - 2.0 * moments)
        joined = joined + jnp.where(upper, term, 0.0)
        combined.append(carry)
    joined = jnp.sum(jnp.sum(joined, axis=0, keepdims=True), axis=1, keepdims=True)
    scalars = jnp.zeros((1, NY), jnp.float32)
    for c in range(COMPS):
        value = own[c] + jnp.where(comp == c, joined, 0.0)
        scalars = jnp.where(lane1 == c, value, scalars)
    for y in range(2):
        back_ref[pl.ds(y, groups, stride=2), :] = jnp.where(upper, combined[y], scalars)


def finish_kernel(cells, rate_ref, got_ref, mass_ref, p_hbm, q_hbm, out_hbm, p_ref, q_ref, out_scr, tab_scr, sems, in_sems):
    blocks = LINES // ROWS
    size = NX * ROWS

    def fetch(k):
        block = pl.ds(k * size, size)
        return (
            pltpu.make_async_copy(p_hbm.at[block, :], p_ref.at[block, :], in_sems.at[0, k]),
            pltpu.make_async_copy(q_hbm.at[block, :], q_ref.at[block, :], in_sems.at[1, k]),
        )

    def copy(k):
        return pltpu.make_async_copy(out_scr.at[pl.ds(k * PITCH, NX), :], out_hbm.at[k], sems.at[k])

    for k in range(blocks):
        for one in fetch(k):
            one.start()
    rate = rate_ref[0]
    index = row_of((NX, NY)).astype(jnp.float32)
    tab_scr[0] = jnp.exp(-rate * (index + 1.0))
    tab_scr[1] = jnp.exp(-rate * (float(NX) - index))
    total = jnp.sum(got_ref[...], axis=0, keepdims=True)
    slot = lane_of((NZ, NY)) // WIDE
    terms = []
    for c in range(COMPS):
        mean_square = pick(mass_ref[0:1, :], c)
        ratio = jnp.sqrt(mean_square / (pick(total, c) / cells + EPS))
        lifted = jnp.broadcast_to(ratio * pick(mass_ref[0:1, :], COMPS + c), (NZ, NY))
        ratio = jnp.broadcast_to(ratio, (NZ, NY))
        forward = jnp.zeros((NZ, NY), jnp.float32)
        backward = jnp.zeros((NZ, NY), jnp.float32)
        for j in range(BLOCKS):
            piece = got_ref[j * LINES + c * NZ : j * LINES + (c + 1) * NZ, :]
            forward = jnp.where(slot == j, pltpu.roll(piece, (WIDE * (j - 2)) % NY, 1) if j != 2 else piece, forward)
            backward = jnp.where(slot == j, pltpu.roll(piece, (WIDE * (j - 3)) % NY, 1) if j != 3 else piece, backward)
        terms.append((ratio[:ROWS], lifted[:ROWS], ratio * forward, ratio * backward))

    for k in range(blocks):
        comp, block = k // (NZ // ROWS), k % (NZ // ROWS)
        ratio, lifted = terms[comp][:2]
        forward, backward = [t[block * ROWS : (block + 1) * ROWS, :] for t in terms[comp][2:]]
        for one in fetch(k):
            one.wait()

        def step(x, _):
            rise = tab_scr[0, pl.ds(x, 1), :]
            fall = tab_scr[1, pl.ds(x, 1), :]
            place = pl.ds(pl.multiple_of(k * size + x * ROWS, ROWS), ROWS)
            value = ratio * p_ref[place, :] + lifted * q_ref[place, :]
            target = pl.ds(k * ROWS * PITCH + x, ROWS, stride=PITCH)
            out_scr[target, :] = value - (rise * forward + fall * backward)
            return 0

        lax.fori_loop(0, NX, step, 0, unroll=16)
        for line in range(ROWS):
            copy(k * ROWS + line).start()
    for line in range(LINES):
        copy(line).wait()


def far(x):
    return pltpu.with_memory_space_constraint(x, pltpu.HBM)


def near(x):
    return pltpu.with_memory_space_constraint(x, pltpu.VMEM)


def f32(*shape):
    return jax.ShapeDtypeStruct(shape, jnp.float32)


def shards(orbitals, potential, shift_ratio):
    groups = lax.axis_size(GX)
    devices = lax.axis_size(ALL)
    cells = float(NZ * NX * NY * devices)
    line_cells = NX * groups
    sigma = shift_ratio / float(line_cells * line_cells)
    rate = jnp.log1p(sigma + jnp.sqrt(sigma * (sigma + 2.0)))
    gain = jnp.sqrt(sigma / (sigma + 2.0))
    me = lax.axis_index(ALL).astype(jnp.int32).reshape(1)
    o = far(orbitals.reshape(LINES, NX, NY))
    cells_all = LINES * NX
    big = pltpu.VMEM((cells_all, NY), jnp.float32)
    spread = pltpu.VMEM((LINES * PITCH, NY), jnp.float32)
    row = pltpu.VMEM((LINES, NY), jnp.float32)
    small = pltpu.VMEM((8, NY), jnp.float32)
    queue = pltpu.SemaphoreType.DMA((LINES,))

    o_near, edge, first, last = pl.pallas_call(
        load_kernel,
        out_shape=(spread, row, row, row),
        in_specs=[HBM],
        out_specs=(VMEM,) * 4,
        scratch_shapes=[queue],
        name="load",
        compiler_params=PARAMS,
    )(o)
    halo = near(lax.ppermute(edge, "gy", [(0, 1), (1, 0)]))
    before = near(lax.ppermute(last, GX, [(i, (i + 1) % groups) for i in range(groups)]))
    o_near, edge, first = near(o_near), near(edge), near(first)

    a, tips, sums = pl.pallas_call(
        gather_kernel,
        out_shape=(big, pltpu.VMEM((8, LINES, NY), jnp.float32), small),
        in_specs=[SMEM, SMEM, SMEM, VMEM, HBM],
        out_specs=(VMEM,) * 3,
        scratch_shapes=[
            pltpu.VMEM((NZ * PITCH, NY), jnp.float32),
            pltpu.VMEM((4, NX, NY), jnp.float32),
            queue,
        ],
        name="gather",
        compiler_params=PARAMS,
    )(rate, gain, sigma, o_near, far(potential))
    a, tips, sums = near(a), near(tips), near(sums)

    msg = pl.pallas_call(
        pack_kernel,
        out_shape=pltpu.VMEM((3 * devices, NY), jnp.float32),
        in_specs=[SMEM, SMEM] + [VMEM] * 6,
        out_specs=VMEM,
        name="pack",
        compiler_params=PARAMS,
    )(rate, gain, tips, sums, edge, halo, first, before)
    got = lax.all_to_all(msg.reshape(devices, 1, 3 * NY), ALL, 0, 0, tiled=True).reshape(3 * devices, NY)

    p, q, local = pl.pallas_call(
        sweep_kernel,
        out_shape=(big, big, small),
        in_specs=[SMEM] * 3 + [HBM] + [VMEM] * 4,
        out_specs=(VMEM,) * 3,
        scratch_shapes=[spread] + [pltpu.VMEM((NX * NZ, NY), jnp.float32)] * 3 + [queue],
        name="sweep",
        compiler_params=PARAMS,
    )(rate, gain, sigma, o, a, edge, halo, sums)
    local = near(local)

    back, mass = pl.pallas_call(
        lambda *refs: owner_kernel(groups, cells, *refs),
        out_shape=(pltpu.VMEM((devices, NY), jnp.float32), small),
        in_specs=[SMEM] * 4 + [VMEM] * 3,
        out_specs=(VMEM,) * 2,
        name="owner",
        compiler_params=PARAMS,
    )(me, rate, gain, sigma, near(got), sums, local)
    returned = lax.all_to_all(back.reshape(devices, 1, NY), ALL, 0, 0, tiled=True).reshape(devices, NY)

    out = pl.pallas_call(
        lambda *refs: finish_kernel(cells, *refs),
        out_shape=f32(LINES, NX, NY),
        in_specs=[SMEM, VMEM, VMEM, HBM, HBM],
        out_specs=HBM,
        scratch_shapes=[
            big,
            big,
            spread,
            pltpu.VMEM((2, NX, NY), jnp.float32),
            queue,
            pltpu.SemaphoreType.DMA((2, LINES // ROWS)),
        ],
        name="finish",
        compiler_params=PARAMS,
    )(rate, near(returned), near(mass), far(p), far(q))
    return out.reshape(orbitals.shape)


def solution(mesh):
    split = Mesh(mesh.devices.reshape(2, 4, 8, 2, mesh.shape["gy"]), ALL)
    return jax.shard_map(
        shards,
        mesh=split,
        in_specs=(P(None, None, GX, "gy"), P(None, GX, "gy"), P()),
        out_specs=P(None, None, GX, "gy"),
        check_vma=False,
    )
```

```python
import jax
import jax.numpy as jnp
from jax import lax
from jax.experimental import pallas as pl
from jax.experimental.pallas import tpu as pltpu
from jax.sharding import Mesh
from jax.sharding import PartitionSpec as P

GX = ("gx_0", "gx_1", "gx_2", "gx_3")
INNER = ("gx_2", "gx_3")
OUTER = ("gx_0", "gx_1", "gy")
ALL = ("gx_0", "gx_1", "gx_2", "gx_3", "gy")

TAU = 4.0
EPS = 1e-06
COUPLING_FIRST = 0.06
COUPLING_SECOND = 0.05
COUPLING_CROSS = 0.04
HIGHEST = lax.Precision.HIGHEST

COMPS = 2
NZ = 32
NX = 64
NY = 128
LINES = COMPS * NZ
MEMBERS = 16
SHARE = LINES // MEMBERS
STRIDE = 8 * SHARE + 1
BACK = 2 * SHARE + 1
PITCH = NX + 8
ROWS = 8

PARAMS = pltpu.CompilerParams(vmem_limit_bytes=16 << 20)
VMEM = pl.BlockSpec(memory_space=pltpu.VMEM)
HBM = pl.BlockSpec(memory_space=pltpu.HBM)
SMEM = pl.BlockSpec(memory_space=pltpu.SMEM)


def lane_of(shape):
    return lax.broadcasted_iota(jnp.int32, shape, 1)


def row_of(shape):
    return lax.broadcasted_iota(jnp.int32, shape, 0)


def rows(x, comp):
    return pl.ds(pl.multiple_of(x * LINES + comp * NZ, NZ), NZ)


def part(comp):
    return slice(comp * NZ, (comp + 1) * NZ)


def start_planes(source, target, sems):
    def copy(k):
        place = pl.ds(pl.multiple_of(k * PITCH, 8), NX)
        return pltpu.make_async_copy(source.at[k], target.at[place, :], sems.at[k])

    def start(k, _):
        copy(k).start()
        return 0

    lax.fori_loop(0, source.shape[0], start, 0, unroll=8)

    def wait(first, last):
        def one(k, _):
            copy(k).wait()
            return 0

        lax.fori_loop(first, last, one, 0, unroll=8)

    return wait


def line_rows(x, comp=0):
    return pl.ds(comp * NZ * PITCH + x, NZ, stride=PITCH)


def load_kernel(o_hbm, v_hbm, o_ref, v_ref, edge_ref, first_ref, last_ref, sems, v_sems):
    wait = start_planes(o_hbm, o_ref, sems)
    wait_v = start_planes(v_hbm, v_ref, v_sems)
    lane = lane_of((NZ, NY)) // 2
    for c in range(COMPS):
        wait(c * NZ, (c + 1) * NZ)

        def step(x, packed):
            return jnp.where(lane == x, pltpu.roll(o_ref[line_rows(x, c), :], 2 * x + 1, 1), packed)

        edge_ref[part(c), :] = lax.fori_loop(0, NX, step, jnp.zeros((NZ, NY), jnp.float32), unroll=8)
        first_ref[part(c), :] = o_ref[line_rows(0, c), :]
        last_ref[part(c), :] = o_ref[line_rows(NX - 1, c), :]
    wait_v(0, NZ)


def tables(rate, count):
    place = (row_of((count * NX, NY)) // count).astype(jnp.float32)
    index = row_of((NX, NY)).astype(jnp.float32)
    rise = jnp.exp(-rate * (index + 1.0))
    fall = jnp.exp(-rate * (float(NX) - index))
    shape = (count * NX, NX)
    gap = (row_of(shape) // count - lane_of(shape)).astype(jnp.float32)
    near = jnp.exp(-rate * jnp.abs(gap))
    return (
        jnp.exp(-rate * (float(NX - 1) - place)),
        jnp.exp(-rate * place),
        dot(near, rise),
        dot(near, fall),
    )


def gather_kernel(rate_ref, gain_ref, sigma_ref, o_ref, v_ref, a_ref, tips_ref, sums_ref, tab_scr):
    rate = rate_ref[0]
    gain4 = TAU * gain_ref[0]
    keep = 1.0 - TAU * sigma_ref[0]
    for k, table in enumerate(tables(rate, 1)):
        tab_scr[k] = table
    zero = jnp.zeros((NZ, NY), jnp.float32)
    decay = jnp.exp(jnp.full((NZ, NY), -rate, jnp.float32))

    def step(x, carry):
        before, cross, square, sums = carry
        o = [o_ref[line_rows(x, c), :] for c in range(COMPS)]
        weights = [tab_scr[k, pl.ds(x, 1), :] for k in range(4)]
        s = [o[0] * o[0], o[1] * o[1]]
        both = COUPLING_CROSS * (s[0] + s[1])
        base = (v_ref[line_rows(x), :] + 2.0) + both
        own = (COUPLING_FIRST - COUPLING_CROSS, COUPLING_SECOND - COUPLING_CROSS)
        new_cross, new_square, new_sums = [], [], []
        for c in range(COMPS):
            around = pltpu.roll(o[c], 1, 0) + pltpu.roll(o[c], NZ - 1, 0)
            around = around + (pltpu.roll(o[c], 1, 1) + pltpu.roll(o[c], NY - 1, 1))
            a = (base + own[c] * s[c]) * o[c] - 0.5 * around
            a_ref[rows(x, c), :] = a
            new_cross.append(cross[c] + o[c] * ((a + o[c]) - before[c]))
            new_square.append(square[c] + s[c])
            new_sums.append(
                [decay * sums[c][0] + o[c], decay * sums[c][1] + a]
                + [sums[c][1 + k] + weights[k] * o[c] for k in range(1, 4)]
                + [sums[c][4 + k] + weights[k] * a for k in range(1, 4)]
            )
        return o, new_cross, new_square, new_sums

    _, cross, square, sums = lax.fori_loop(
        0, NX, step, ([zero] * 2, [zero] * 2, [zero] * 2, [[zero] * 8] * 2), unroll=2
    )
    once = jnp.exp(jnp.full((NZ, NY), -rate, jnp.float32))
    for c in range(COMPS):
        f_o, f_a, b_o, r_o, s_o, b_a, r_a, s_a = sums[c]
        tips_ref[0, part(c), :] = f_o
        tips_ref[1, part(c), :] = b_o
        tips_ref[2, part(c), :] = f_a
        tips_ref[3, part(c), :] = b_a
        tips_ref[4, part(c), :] = gain4 * r_o
        tips_ref[5, part(c), :] = gain4 * s_o
        tips_ref[6, part(c), :] = keep * (once * b_o) - gain4 * r_a
        tips_ref[7, part(c), :] = keep * (once * f_o) - gain4 * s_a
        sums_ref[c : c + 1, :] = jnp.sum(cross[c], axis=0, keepdims=True)
        sums_ref[COMPS + c : COMPS + c + 1, :] = jnp.sum(square[c], axis=0, keepdims=True)


def local_shift(sums_ref, c, sigma):
    cross = jnp.sum(sums_ref[c : c + 1, :], axis=1, keepdims=True)
    square = jnp.sum(sums_ref[COMPS + c : COMPS + c + 1, :], axis=1, keepdims=True)
    return cross / (square + EPS) + sigma


def sweep_kernel(rate_ref, gain_ref, sigma_ref, o_hbm, a_ref, edge_ref, halo_ref, sums_ref, p_hbm, q_hbm, local_ref, p_ref, q_ref, o_ref, fo_scr, fa_scr, a_scr, sems, out_sems):
    wait = start_planes(o_hbm, o_ref, sems)

    def send(c):
        block = pl.ds(c * NZ * NX, NZ * NX)
        return (
            pltpu.make_async_copy(p_ref.at[block, :], p_hbm.at[block, :], out_sems.at[0, c]),
            pltpu.make_async_copy(q_ref.at[block, :], q_hbm.at[block, :], out_sems.at[1, c]),
        )

    gain4 = TAU * gain_ref[0]
    keep = 1.0 - TAU * sigma_ref[0]
    decay = jnp.exp(jnp.full((NZ, NY), -rate_ref[0], jnp.float32))
    lane = lane_of((NZ, NY))
    zero = jnp.zeros((NZ, NY), jnp.float32)
    lane1 = lane_of((1, NY))
    for c in range(COMPS):
        delta = -0.5 * (halo_ref[part(c), :] - edge_ref[part(c), :])
        even = lane % 2 == 0
        delta = jnp.where(even, pltpu.roll(delta, NY - 1, 1), pltpu.roll(delta, 1, 1))
        ends = (lane == 0) | (lane == NY - 1)

        def ahead(x, carry):
            fo, fa = carry
            o = o_ref[line_rows(x, c), :]
            a = a_ref[rows(x, c), :] + jnp.where(ends, pltpu.roll(delta, NY - (2 * x + 1), 1), 0.0)
            fo = decay * fo + o
            fa = decay * fa + a
            fo_scr[pl.ds(pl.multiple_of(x * NZ, NZ), NZ), :] = fo
            fa_scr[pl.ds(pl.multiple_of(x * NZ, NZ), NZ), :] = fa
            a_scr[pl.ds(pl.multiple_of(x * NZ, NZ), NZ), :] = a
            return fo, fa

        wait(c * NZ, (c + 1) * NZ)
        lax.fori_loop(0, NX, ahead, (zero, zero), unroll=4)
        shift = jnp.broadcast_to(local_shift(sums_ref, c, sigma_ref[0]), (NZ, NY))

        def behind(k, carry):
            x = NX - 1 - k
            bo, ba, ww, wq, qq = carry
            o, a = o_ref[line_rows(x, c), :], a_scr[pl.ds(pl.multiple_of(x * NZ, NZ), NZ), :]
            do, da = decay * bo, decay * ba
            q = gain4 * (fo_scr[pl.ds(pl.multiple_of(x * NZ, NZ), NZ), :] + do)
            p = keep * o - gain4 * (fa_scr[pl.ds(pl.multiple_of(x * NZ, NZ), NZ), :] + da)
            for b in range(NZ // ROWS):
                place = pl.ds(pl.multiple_of(((c * NZ // ROWS + b) * NX + x) * ROWS, ROWS), ROWS)
                q_ref[place, :] = q[b * ROWS : (b + 1) * ROWS, :]
                p_ref[place, :] = p[b * ROWS : (b + 1) * ROWS, :]
            w = p + shift * q
            return do + o, da + a, ww + w * w, wq + w * q, qq + q * q

        _, _, ww, wq, qq = lax.fori_loop(0, NX, behind, (zero,) * 5, unroll=4)
        for k, value in enumerate((ww, wq, qq)):
            local_ref[3 * c + k : 3 * c + k + 1, :] = jnp.sum(value, axis=0, keepdims=True)
        for one in send(c):
            one.start()
    for c in range(COMPS):
        for one in send(c):
            one.wait()


def dot(a, b):
    return jnp.dot(a, b, precision=HIGHEST, preferred_element_type=jnp.float32)


def pack_kernel(rate_ref, gain_ref, tips_ref, sums_ref, edge_ref, halo_ref, first_ref, before_ref, msg_ref):
    gain4 = TAU * gain_ref[0]
    halo = halo_ref[...]
    delta = -0.5 * (halo - edge_ref[...])
    shape = (NY, NY)
    odd = row_of(shape) % 2
    hit = ((lane_of(shape) == 0) & (odd == 0)) | ((lane_of(shape) == NY - 1) & (odd == 1))
    fixes = [dot(delta, jnp.where(hit, table, 0.0)) for table in tables(rate_ref[0], 2)]
    tips = [tips_ref[k] for k in range(8)]
    tips[2] = tips[2] + fixes[0]
    tips[3] = tips[3] + fixes[1]
    tips[6] = tips[6] - gain4 * fixes[2]
    tips[7] = tips[7] - gain4 * fixes[3]

    lane = lane_of((LINES, NY))
    even = lane % 2 == 0
    swapped = jnp.where(even, pltpu.roll(delta, NY - 1, 1), pltpu.roll(delta, 1, 1))
    extra = edge_ref[...] * swapped - first_ref[...] * before_ref[...]
    row_lane = lane_of((1, NY))
    scalars = jnp.zeros((1, NY), jnp.float32)
    for c in range(COMPS):
        cross = sums_ref[c : c + 1, :] + jnp.sum(extra[c * NZ : (c + 1) * NZ, :], axis=0, keepdims=True)
        scalars = jnp.where(row_lane == c, jnp.sum(cross, axis=1, keepdims=True), scalars)
        square = jnp.sum(sums_ref[COMPS + c : COMPS + c + 1, :], axis=1, keepdims=True)
        scalars = jnp.where(row_lane == COMPS + c, square, scalars)
    for f in range(MEMBERS):
        base = STRIDE * f
        for k in range(8):
            msg_ref[base + SHARE * k : base + SHARE * (k + 1), :] = tips[k][SHARE * f : SHARE * (f + 1), :]
        msg_ref[base + 8 * SHARE : base + 8 * SHARE + 1, :] = scalars


def pick(vector, k):
    return jnp.sum(jnp.where(lane_of((1, NY)) == k, vector, 0.0), axis=1, keepdims=True)


def total_of(block):
    return jnp.sum(jnp.sum(block, axis=0, keepdims=True), axis=1, keepdims=True)


def scalar_row(values):
    lane = lane_of((1, NY))
    row = jnp.zeros((1, NY), jnp.float32)
    for k, value in enumerate(values):
        row = jnp.where(lane == k, value, row)
    return row


def overlap(rate, count):
    shape = (8, NY)
    index = (row_of(shape) * NY + lane_of(shape) + 1).astype(jnp.float32)
    rho = total_of(jnp.where(index <= float(count), jnp.exp(-2.0 * rate * index), 0.0))
    omega = float(count) * jnp.exp(jnp.full((1, 1), -rate * float(count + 1), jnp.float32))
    return rho, omega


def other_half(x):
    return pltpu.roll(x, SHARE, 0)


def reach(rate, f, upper):
    steps = jnp.where(upper, float(f), float(MEMBERS - 1 - f))
    return jnp.exp(-rate * float(NX) * steps)


def group_kernel(member_ref, rate_ref, gain_ref, sigma_ref, got_ref, sums_ref, local_ref, msg_ref, pre_ref):
    rate, sigma = rate_ref[0], sigma_ref[0]
    gain4 = TAU * gain_ref[0]
    shape = (2 * SHARE, NY)
    upper = row_of(shape) < SHARE
    block = jnp.exp(jnp.full(shape, -rate * float(NX), jnp.float32))
    rho, omega = overlap(rate, NX)
    zero = jnp.zeros(shape, jnp.float32)

    def piece(f, k):
        start = STRIDE * f + 2 * SHARE * k
        return got_ref[start : start + 2 * SHARE, :]

    total = got_ref[STRIDE - 1 : STRIDE, :]
    for f in range(1, MEMBERS):
        total = total + got_ref[STRIDE * (f + 1) - 1 : STRIDE * (f + 1), :]
    sums = [pick(total, k) for k in range(2 * COMPS)]
    shifts = [sums[c] / (sums[COMPS + c] + EPS) + sigma for c in range(COMPS)]
    shift = jnp.where(member_ref[0] * SHARE < NZ, shifts[0], shifts[1])

    tips = [[piece(f, k) for f in range(MEMBERS)] for k in range(2)]
    ends, before = [], []
    for k in range(2):
        forward, backward = [zero], [zero]
        for f in range(MEMBERS):
            forward.append(block * forward[-1] + tips[k][f])
            backward.append(block * backward[-1] + tips[k][MEMBERS - 1 - f])
        ends.append(jnp.where(upper, forward[-1], backward[-1]))
        before.append([jnp.where(upper, forward[f], backward[MEMBERS - 1 - f]) for f in range(MEMBERS)])
    moment0, moment1, ww, wq, qq = (zero,) * 5
    for f in range(MEMBERS):
        pre_o, pre_a = gain4 * before[0][f], gain4 * before[1][f]
        pre_ref[4 * SHARE * f : 4 * SHARE * f + 2 * SHARE, :] = pre_o
        pre_ref[4 * SHARE * f + 2 * SHARE : 4 * SHARE * (f + 1), :] = pre_a
        own_q, own_p = piece(f, 2), piece(f, 3)
        weight = reach(rate, f, upper)
        spread_o = rho * pre_o + omega * other_half(pre_o)
        spread_a = rho * pre_a + omega * other_half(pre_a)
        moment0 = moment0 + weight * (own_p - spread_a)
        moment1 = moment1 + weight * (own_q + spread_o)
        y = pre_a - shift * pre_o
        spread_y = spread_a - shift * spread_o
        own_w = own_p + shift * own_q
        ww = ww + y * (spread_y - 2.0 * own_w)
        wq = wq + (pre_o * (own_w - spread_y) - y * own_q)
        qq = qq + pre_o * (2.0 * own_q + spread_o)
    values = list(sums)
    for c in range(COMPS):
        values += [jnp.sum(local_ref[3 * c + k : 3 * c + k + 1, :], axis=1, keepdims=True) for k in range(3)]
        values.append(local_shift(sums_ref, c, sigma))
    values += [total_of(ww), total_of(wq), total_of(qq), shift]
    scalars = scalar_row(values)
    for k in range(MEMBERS):
        for i, value in enumerate((gain4 * ends[0], gain4 * ends[1], moment1, moment0)):
            start = STRIDE * k + 2 * SHARE * i
            msg_ref[start : start + 2 * SHARE, :] = value
        msg_ref[STRIDE * (k + 1) - 1 : STRIDE * (k + 1), :] = scalars


def owner_kernel(groups, cells, member_ref, mine_ref, rate_ref, sigma_ref, got_ref, pre_ref, back_ref, mass_ref):
    rate, sigma = rate_ref[0], sigma_ref[0]
    member, mine = member_ref[0], mine_ref[0]
    shape = (2 * SHARE, NY)
    upper = row_of(shape) < SHARE
    span = NX * MEMBERS
    block = jnp.exp(jnp.full(shape, -rate * float(span), jnp.float32))
    wrap = 1.0 - jnp.exp(jnp.full(shape, -rate * float(span * groups), jnp.float32))
    rho, omega = overlap(rate, span)
    scal = got_ref[pl.ds(STRIDE - 1, 2 * groups, stride=STRIDE), :]
    lane = lane_of((2 * groups, NY))

    def column(k):
        return jnp.sum(jnp.where(lane == k, scal, 0.0), axis=1, keepdims=True)

    def expand(first, value):
        ww, wq, qq, base = [column(first + k) for k in range(4)]
        more = value - base
        return jnp.sum(ww + more * (2.0 * wq + more * qq), axis=0, keepdims=True)

    total = jnp.sum(scal, axis=0, keepdims=True)
    squares, shifts = [], []
    for c in range(COMPS):
        mean_square = pick(total, COMPS + c) / cells
        squares.append(mean_square)
        shifts.append((pick(total, c) / cells) / (mean_square + EPS) + sigma)
    mass_ref[...] = jnp.broadcast_to(scalar_row(squares + shifts), (8, NY))
    first = member * SHARE < NZ
    shift = jnp.where(first, shifts[0], shifts[1])

    def piece(g, y, k):
        start = STRIDE * (2 * g + y) + 2 * SHARE * k
        return got_ref[start : start + 2 * SHARE, :]

    zero = jnp.zeros(shape, jnp.float32)
    acc, chosen = zero, zero
    for y in range(2):
        ends = [piece(g, y, 1) - shift * piece(g, y, 0) for g in range(groups)]
        forward, backward = zero, zero
        for g in range(groups):
            forward = block * forward + ends[g]
            backward = block * backward + ends[groups - 1 - g]
        entering_f, entering_b = [forward / wrap], [backward / wrap]
        for g in range(groups - 1):
            entering_f.append(block * entering_f[-1] + ends[g])
            entering_b.append(block * entering_b[-1] + ends[groups - 1 - g])
        for g in range(groups):
            carry = jnp.where(upper, entering_f[g], entering_b[groups - 1 - g])
            moment = piece(g, y, 3) + shift * piece(g, y, 2)
            acc = acc + carry * (rho * carry + omega * other_half(carry) - 2.0 * moment)
            chosen = jnp.where(mine == 2 * g + y, carry, chosen)
    joined = total_of(acc) + expand(12, shift)
    values = []
    for c in range(COMPS):
        value = expand(4 + 4 * c, shifts[c])
        values.append(value + jnp.where(first == (c == 0), joined, 0.0))
    scalars = scalar_row(values)
    for f in range(MEMBERS):
        pre_o = pre_ref[4 * SHARE * f : 4 * SHARE * f + 2 * SHARE, :]
        pre_a = pre_ref[4 * SHARE * f + 2 * SHARE : 4 * SHARE * (f + 1), :]
        value = (pre_a - shift * pre_o) + reach(rate, f, upper) * chosen
        back_ref[BACK * f : BACK * f + 2 * SHARE, :] = value
        back_ref[BACK * (f + 1) - 1 : BACK * (f + 1), :] = scalars


def blend_kernel(mass_ref, p_hbm, q_hbm, w_ref, p_ref, q_ref, sems):
    size = NX * ROWS

    def fetch(k):
        block = pl.ds(k * size, size)
        return (
            pltpu.make_async_copy(p_hbm.at[block, :], p_ref.at[block, :], sems.at[0, k]),
            pltpu.make_async_copy(q_hbm.at[block, :], q_ref.at[block, :], sems.at[1, k]),
        )

    for k in range(LINES // ROWS):
        for one in fetch(k):
            one.start()
    for k in range(LINES // ROWS):
        comp = k * ROWS // NZ
        shift = jnp.broadcast_to(pick(mass_ref[0:1, :], COMPS + comp), (NX, NY))
        for one in fetch(k):
            one.wait()

        def step(i, _):
            place = pl.ds(pl.multiple_of(k * size + i * NX, NX), NX)
            w_ref[place, :] = p_ref[place, :] + shift * q_ref[place, :]
            return 0

        lax.fori_loop(0, ROWS, step, 0, unroll=2)


def finish_kernel(cells, rate_ref, got_ref, mass_ref, w_ref, out_hbm, out_scr, tab_scr, sems):
    blocks = LINES // ROWS
    size = NX * ROWS

    def copy(k):
        return pltpu.make_async_copy(out_scr.at[pl.ds(k * PITCH, NX), :], out_hbm.at[k], sems.at[k])

    rate = rate_ref[0]
    index = row_of((NX, NY)).astype(jnp.float32)
    tab_scr[0] = jnp.exp(-rate * (index + 1.0))
    tab_scr[1] = jnp.exp(-rate * (float(NX) - index))
    total = got_ref[BACK - 1 : BACK, :]
    for f in range(1, MEMBERS):
        total = total + got_ref[BACK * (f + 1) - 1 : BACK * (f + 1), :]
    scales = []
    for c in range(COMPS):
        mean_square = pick(mass_ref[0:1, :], c)
        ratio = jnp.sqrt(mean_square / (pick(total, c) / cells + EPS))
        scales.append(jnp.broadcast_to(ratio, (ROWS, NY)))

    def carries(k, half):
        members = range(k * ROWS // SHARE, (k + 1) * ROWS // SHARE)
        starts = [BACK * f + half * SHARE for f in members]
        return jnp.concatenate([got_ref[i : i + SHARE, :] for i in starts], axis=0)

    for k in range(blocks):
        comp = k * ROWS // NZ
        ratio = scales[comp]
        forward, backward = ratio * carries(k, 0), ratio * carries(k, 1)
        def step(x, _):
            rise = tab_scr[0, pl.ds(x, 1), :]
            fall = tab_scr[1, pl.ds(x, 1), :]
            place = pl.ds(pl.multiple_of(k * size + x * ROWS, ROWS), ROWS)
            value = ratio * w_ref[place, :]
            target = pl.ds(k * ROWS * PITCH + x, ROWS, stride=PITCH)
            out_scr[target, :] = value - (rise * forward + fall * backward)
            return 0

        lax.fori_loop(0, NX, step, 0, unroll=16)
        for line in range(ROWS):
            copy(k * ROWS + line).start()
    for line in range(LINES):
        copy(line).wait()


def far(x):
    return pltpu.with_memory_space_constraint(x, pltpu.HBM)


def near(x):
    return pltpu.with_memory_space_constraint(x, pltpu.VMEM)


def exchange(x, axes):
    peers = lax.axis_size(axes)
    moved = lax.all_to_all(x.reshape(peers, 1, x.size // peers), axes, 0, 0, tiled=True)
    return moved.reshape(x.shape)


def f32(*shape):
    return jax.ShapeDtypeStruct(shape, jnp.float32)


def shards(orbitals, potential, shift_ratio):
    groups = lax.axis_size(GX)
    devices = lax.axis_size(ALL)
    cells = float(NZ * NX * NY * devices)
    line_cells = NX * groups
    sigma = shift_ratio / float(line_cells * line_cells)
    rate = jnp.log1p(sigma + jnp.sqrt(sigma * (sigma + 2.0)))
    gain = jnp.sqrt(sigma / (sigma + 2.0))
    member = lax.axis_index(INNER).astype(jnp.int32)
    mine = lax.axis_index(OUTER).astype(jnp.int32)
    o = far(orbitals.reshape(LINES, NX, NY))
    cells_all = LINES * NX
    big = pltpu.VMEM((cells_all, NY), jnp.float32)
    distant = pltpu.HBM((cells_all, NY), jnp.float32)
    spread = pltpu.VMEM((LINES * PITCH, NY), jnp.float32)
    row = pltpu.VMEM((LINES, NY), jnp.float32)
    small = pltpu.VMEM((8, NY), jnp.float32)
    queue = pltpu.SemaphoreType.DMA((LINES,))

    o_near, v_near, edge, first, last = pl.pallas_call(
        load_kernel,
        out_shape=(spread, pltpu.VMEM((NZ * PITCH, NY), jnp.float32), row, row, row),
        in_specs=[HBM] * 2,
        out_specs=(VMEM,) * 5,
        scratch_shapes=[queue, pltpu.SemaphoreType.DMA((NZ,))],
        name="load",
        compiler_params=PARAMS,
    )(o, far(potential))
    halo = near(lax.ppermute(edge, "gy", [(0, 1), (1, 0)]))
    before = near(lax.ppermute(last, GX, [(i, (i + 1) % groups) for i in range(groups)]))
    o_near, edge, first = near(o_near), near(edge), near(first)

    a, tips, sums = pl.pallas_call(
        gather_kernel,
        out_shape=(big, pltpu.VMEM((8, LINES, NY), jnp.float32), small),
        in_specs=[SMEM, SMEM, SMEM, VMEM, VMEM],
        out_specs=(VMEM,) * 3,
        scratch_shapes=[pltpu.VMEM((4, NX, NY), jnp.float32)],
        name="gather",
        compiler_params=PARAMS,
    )(rate, gain, sigma, o_near, near(v_near))
    a, tips, sums = near(a), near(tips), near(sums)

    msg = pl.pallas_call(
        pack_kernel,
        out_shape=pltpu.VMEM((MEMBERS * STRIDE, NY), jnp.float32),
        in_specs=[SMEM, SMEM] + [VMEM] * 6,
        out_specs=VMEM,
        name="pack",
        compiler_params=PARAMS,
    )(rate, gain, tips, sums, edge, halo, first, before)
    got = exchange(msg, INNER)

    p, q, local = pl.pallas_call(
        sweep_kernel,
        out_shape=(distant, distant, small),
        in_specs=[SMEM] * 3 + [HBM] + [VMEM] * 4,
        out_specs=(HBM, HBM, VMEM),
        scratch_shapes=[big, big, spread]
        + [pltpu.VMEM((NX * NZ, NY), jnp.float32)] * 3
        + [queue, pltpu.SemaphoreType.DMA((2, COMPS))],
        name="sweep",
        compiler_params=PARAMS,
    )(rate, gain, sigma, o, a, edge, halo, sums)
    p, q, local = far(p), far(q), near(local)

    joint, pre = pl.pallas_call(
        group_kernel,
        out_shape=(
            pltpu.VMEM((MEMBERS * STRIDE, NY), jnp.float32),
            pltpu.VMEM((4 * SHARE * MEMBERS, NY), jnp.float32),
        ),
        in_specs=[SMEM] * 4 + [VMEM] * 3,
        out_specs=(VMEM,) * 2,
        name="group",
        compiler_params=PARAMS,
    )(member.reshape(1), rate, gain, sigma, near(got), sums, local)
    outer = exchange(joint, OUTER)

    back, mass = pl.pallas_call(
        lambda *refs: owner_kernel(groups // MEMBERS, cells, *refs),
        out_shape=(pltpu.VMEM((MEMBERS * BACK, NY), jnp.float32), small),
        in_specs=[SMEM] * 4 + [VMEM] * 2,
        out_specs=(VMEM,) * 2,
        name="owner",
        compiler_params=PARAMS,
    )(member.reshape(1), mine.reshape(1), rate, sigma, near(outer), near(pre))
    returned = exchange(back, INNER)

    mass = near(mass)
    w = pl.pallas_call(
        blend_kernel,
        out_shape=big,
        in_specs=[VMEM, HBM, HBM],
        out_specs=VMEM,
        scratch_shapes=[big, big, pltpu.SemaphoreType.DMA((2, LINES // ROWS))],
        name="blend",
        compiler_params=PARAMS,
    )(mass, p, q)

    out = pl.pallas_call(
        lambda *refs: finish_kernel(cells, *refs),
        out_shape=f32(LINES, NX, NY),
        in_specs=[SMEM, VMEM, VMEM, VMEM],
        out_specs=HBM,
        scratch_shapes=[spread, pltpu.VMEM((2, NX, NY), jnp.float32), queue],
        name="finish",
        compiler_params=PARAMS,
    )(rate, near(returned), mass, near(w))
    return out.reshape(orbitals.shape)


def solution(mesh):
    split = Mesh(mesh.devices.reshape(2, 4, 8, 2, mesh.shape["gy"]), ALL)
    return jax.shard_map(
        shards,
        mesh=split,
        in_specs=(P(None, None, GX, "gy"), P(None, GX, "gy"), P()),
        out_specs=P(None, None, GX, "gy"),
        check_vma=False,
    )
```

```python
import jax
import jax.numpy as jnp
from jax import lax
from jax.experimental import pallas as pl
from jax.experimental.pallas import tpu as pltpu
from jax.sharding import Mesh
from jax.sharding import PartitionSpec as P

GX = ("gx_0", "gx_1", "gx_2", "gx_3")
INNER = ("gx_2", "gx_3")
OUTER = ("gx_0", "gx_1", "gy")
ALL = ("gx_0", "gx_1", "gx_2", "gx_3", "gy")

TAU = 4.0
EPS = 1e-06
COUPLING_FIRST = 0.06
COUPLING_SECOND = 0.05
COUPLING_CROSS = 0.04
HIGHEST = lax.Precision.HIGHEST

COMPS = 2
NZ = 32
NX = 64
NY = 128
LINES = COMPS * NZ
MEMBERS = 16
SHARE = LINES // MEMBERS
STRIDE = 8 * SHARE + 1
BACK = 2 * SHARE + 1
PITCH = NX + 8
ROWS = 8
UNROLL = 8

PARAMS = pltpu.CompilerParams(vmem_limit_bytes=16 << 20)
VMEM = pl.BlockSpec(memory_space=pltpu.VMEM)
HBM = pl.BlockSpec(memory_space=pltpu.HBM)
SMEM = pl.BlockSpec(memory_space=pltpu.SMEM)


def lane_of(shape):
    return lax.broadcasted_iota(jnp.int32, shape, 1)


def row_of(shape):
    return lax.broadcasted_iota(jnp.int32, shape, 0)


def rows(x, comp):
    return pl.ds(pl.multiple_of(x * LINES + comp * NZ, NZ), NZ)


def part(comp):
    return slice(comp * NZ, (comp + 1) * NZ)


def start_planes(source, target, sems):
    def copy(k):
        place = pl.ds(pl.multiple_of(k * PITCH, 8), NX)
        return pltpu.make_async_copy(source.at[k], target.at[place, :], sems.at[k])

    def start(k, _):
        copy(k).start()
        return 0

    lax.fori_loop(0, source.shape[0], start, 0, unroll=8)

    def wait(first, last):
        def one(k, _):
            copy(k).wait()
            return 0

        lax.fori_loop(first, last, one, 0, unroll=8)

    return wait


def line_rows(x, comp=0):
    return pl.ds(comp * NZ * PITCH + x, NZ, stride=PITCH)


def load_kernel(o_hbm, v_hbm, o_ref, v_ref, edge_ref, first_ref, last_ref, sems, v_sems):
    wait = start_planes(o_hbm, o_ref, sems)
    lane = lane_of((NZ, NY)) // 2
    for c in range(COMPS):
        wait(c * NZ, (c + 1) * NZ)
        if c == 0:
            wait_v = start_planes(v_hbm, v_ref, v_sems)

        def step(x, packed):
            return jnp.where(lane == x, pltpu.roll(o_ref[line_rows(x, c), :], 2 * x + 1, 1), packed)

        edge_ref[part(c), :] = lax.fori_loop(0, NX, step, jnp.zeros((NZ, NY), jnp.float32), unroll=16)
        first_ref[part(c), :] = o_ref[line_rows(0, c), :]
        last_ref[part(c), :] = o_ref[line_rows(NX - 1, c), :]
    wait_v(0, NZ)


def tables(rate, count):
    place = (row_of((count * NX, NY)) // count).astype(jnp.float32)
    index = row_of((NX, NY)).astype(jnp.float32)
    rise = jnp.exp(-rate * (index + 1.0))
    fall = jnp.exp(-rate * (float(NX) - index))
    shape = (count * NX, NX)
    gap = (row_of(shape) // count - lane_of(shape)).astype(jnp.float32)
    near = jnp.exp(-rate * jnp.abs(gap))
    return (
        jnp.exp(-rate * (float(NX - 1) - place)),
        jnp.exp(-rate * place),
        dot(near, rise),
        dot(near, fall),
    )


def gather_kernel(rate_ref, gain_ref, sigma_ref, o_ref, v_ref, a_ref, tips_ref, sums_ref, tab_scr):
    rate = rate_ref[0]
    gain4 = TAU * gain_ref[0]
    keep = 1.0 - TAU * sigma_ref[0]
    for k, table in enumerate(tables(rate, 1)):
        tab_scr[k] = table
    zero = jnp.zeros((NZ, NY), jnp.float32)
    decay = jnp.exp(jnp.full((NZ, NY), -rate, jnp.float32))

    def fold(total, block):
        for b in range(NZ // ROWS):
            total = total + block[b * ROWS : (b + 1) * ROWS, :]
        return total

    def around_of(o):
        near_z = pltpu.roll(o, 1, 0) + pltpu.roll(o, NZ - 1, 0)
        return -0.5 * (near_z + (pltpu.roll(o, 1, 1) + pltpu.roll(o, NY - 1, 1)))

    def read(x):
        o = [o_ref[line_rows(x, c), :] for c in range(COMPS)]
        return o, [around_of(one) for one in o]

    def step(x, carry):
        before, o, around, cross, square = carry
        after = read(jnp.minimum(x + 1, NX - 1))
        s = [o[0] * o[0], o[1] * o[1]]
        both = COUPLING_CROSS * (s[0] + s[1])
        base = (v_ref[line_rows(x), :] + 2.0) + both
        own = (COUPLING_FIRST - COUPLING_CROSS, COUPLING_SECOND - COUPLING_CROSS)
        new_cross, new_square = [], []
        for c in range(COMPS):
            a = (base + own[c] * s[c]) * o[c] + around[c]
            a_ref[rows(x, c), :] = a
            new_cross.append(fold(cross[c], o[c] * ((a + o[c]) - before[c])))
            new_square.append(fold(square[c], s[c]))
        return o, after[0], after[1], new_cross, new_square

    part_sum = [jnp.zeros((ROWS, NY), jnp.float32)] * 2
    start = read(0)
    cross, square = lax.fori_loop(0, NX, step, ([zero] * 2, *start, part_sum, part_sum), unroll=UNROLL)[3:]

    sums = []
    for c in range(COMPS):
        def add(x, sums):
            o, a = o_ref[line_rows(x, c), :], a_ref[rows(x, c), :]
            weights = [tab_scr[k, pl.ds(x, 1), :] for k in range(4)]
            return (
                [decay * sums[0] + o, decay * sums[1] + a]
                + [sums[1 + k] + weights[k] * o for k in range(1, 4)]
                + [sums[4 + k] + weights[k] * a for k in range(1, 4)]
            )

        sums.append(lax.fori_loop(0, NX, add, [zero] * 8, unroll=8))
    once = jnp.exp(jnp.full((NZ, NY), -rate, jnp.float32))
    for c in range(COMPS):
        f_o, f_a, b_o, r_o, s_o, b_a, r_a, s_a = sums[c]
        tips_ref[0, part(c), :] = f_o
        tips_ref[1, part(c), :] = b_o
        tips_ref[2, part(c), :] = f_a
        tips_ref[3, part(c), :] = b_a
        tips_ref[4, part(c), :] = gain4 * r_o
        tips_ref[5, part(c), :] = gain4 * s_o
        tips_ref[6, part(c), :] = keep * (once * b_o) - gain4 * r_a
        tips_ref[7, part(c), :] = keep * (once * f_o) - gain4 * s_a
        sums_ref[c : c + 1, :] = jnp.sum(cross[c], axis=0, keepdims=True)
        sums_ref[COMPS + c : COMPS + c + 1, :] = jnp.sum(square[c], axis=0, keepdims=True)


def local_shift(sums_ref, c, sigma):
    cross = jnp.sum(sums_ref[c : c + 1, :], axis=1, keepdims=True)
    square = jnp.sum(sums_ref[COMPS + c : COMPS + c + 1, :], axis=1, keepdims=True)
    return cross / (square + EPS) + sigma


def sweep_kernel(rate_ref, gain_ref, sigma_ref, o_hbm, a_ref, edge_ref, halo_ref, sums_ref, p_hbm, q_hbm, local_ref, p_ref, q_ref, o_ref, fo_scr, fa_scr, a_scr, sems, out_sems):
    wait = start_planes(o_hbm, o_ref, sems)

    def send(c):
        block = pl.ds(c * NZ * NX, NZ * NX)
        return (
            pltpu.make_async_copy(p_ref.at[block, :], p_hbm.at[block, :], out_sems.at[0, c]),
            pltpu.make_async_copy(q_ref.at[block, :], q_hbm.at[block, :], out_sems.at[1, c]),
        )

    gain4 = TAU * gain_ref[0]
    keep = 1.0 - TAU * sigma_ref[0]
    decay = jnp.exp(jnp.full((NZ, NY), -rate_ref[0], jnp.float32))
    lane = lane_of((NZ, NY))
    zero = jnp.zeros((NZ, NY), jnp.float32)
    lane1 = lane_of((1, NY))
    for c in range(COMPS):
        delta = -0.5 * (halo_ref[part(c), :] - edge_ref[part(c), :])
        even = lane % 2 == 0
        delta = jnp.where(even, pltpu.roll(delta, NY - 1, 1), pltpu.roll(delta, 1, 1))
        ends = (lane == 0) | (lane == NY - 1)

        def ahead(x, carry):
            fo, fa = carry
            o = o_ref[line_rows(x, c), :]
            a = a_ref[rows(x, c), :] + jnp.where(ends, pltpu.roll(delta, NY - (2 * x + 1), 1), 0.0)
            fo = decay * fo + o
            fa = decay * fa + a
            fo_scr[pl.ds(pl.multiple_of(x * NZ, NZ), NZ), :] = fo
            fa_scr[pl.ds(pl.multiple_of(x * NZ, NZ), NZ), :] = fa
            a_scr[pl.ds(pl.multiple_of(x * NZ, NZ), NZ), :] = a
            return fo, fa

        wait(c * NZ, (c + 1) * NZ)
        lax.fori_loop(0, NX, ahead, (zero, zero), unroll=8)
        shift = jnp.broadcast_to(local_shift(sums_ref, c, sigma_ref[0]), (NZ, NY))

        def behind(k, carry):
            x = NX - 1 - k
            bo, ba, ww, wq, qq = carry
            o, a = o_ref[line_rows(x, c), :], a_scr[pl.ds(pl.multiple_of(x * NZ, NZ), NZ), :]
            do, da = decay * bo, decay * ba
            q = gain4 * (fo_scr[pl.ds(pl.multiple_of(x * NZ, NZ), NZ), :] + do)
            p = keep * o - gain4 * (fa_scr[pl.ds(pl.multiple_of(x * NZ, NZ), NZ), :] + da)
            for b in range(NZ // ROWS):
                place = pl.ds(pl.multiple_of(((c * NZ // ROWS + b) * NX + x) * ROWS, ROWS), ROWS)
                q_ref[place, :] = q[b * ROWS : (b + 1) * ROWS, :]
                p_ref[place, :] = p[b * ROWS : (b + 1) * ROWS, :]
            w = p + shift * q
            return do + o, da + a, ww + w * w, wq + w * q, qq + q * q

        _, _, ww, wq, qq = lax.fori_loop(0, NX, behind, (zero,) * 5, unroll=8)
        for k, value in enumerate((ww, wq, qq)):
            local_ref[3 * c + k : 3 * c + k + 1, :] = jnp.sum(value, axis=0, keepdims=True)
        for one in send(c):
            one.start()
    for c in range(COMPS):
        for one in send(c):
            one.wait()


def dot(a, b):
    return jnp.dot(a, b, precision=HIGHEST, preferred_element_type=jnp.float32)


def pack_kernel(rate_ref, gain_ref, tips_ref, sums_ref, edge_ref, halo_ref, first_ref, before_ref, msg_ref):
    gain4 = TAU * gain_ref[0]
    halo = halo_ref[...]
    delta = -0.5 * (halo - edge_ref[...])
    shape = (NY, NY)
    odd = row_of(shape) % 2
    hit = ((lane_of(shape) == 0) & (odd == 0)) | ((lane_of(shape) == NY - 1) & (odd == 1))
    fixes = [dot(delta, jnp.where(hit, table, 0.0)) for table in tables(rate_ref[0], 2)]
    tips = [tips_ref[k] for k in range(8)]
    tips[2] = tips[2] + fixes[0]
    tips[3] = tips[3] + fixes[1]
    tips[6] = tips[6] - gain4 * fixes[2]
    tips[7] = tips[7] - gain4 * fixes[3]

    lane = lane_of((LINES, NY))
    even = lane % 2 == 0
    swapped = jnp.where(even, pltpu.roll(delta, NY - 1, 1), pltpu.roll(delta, 1, 1))
    extra = edge_ref[...] * swapped - first_ref[...] * before_ref[...]
    row_lane = lane_of((1, NY))
    scalars = jnp.zeros((1, NY), jnp.float32)
    for c in range(COMPS):
        cross = sums_ref[c : c + 1, :] + jnp.sum(extra[c * NZ : (c + 1) * NZ, :], axis=0, keepdims=True)
        scalars = jnp.where(row_lane == c, jnp.sum(cross, axis=1, keepdims=True), scalars)
        square = jnp.sum(sums_ref[COMPS + c : COMPS + c + 1, :], axis=1, keepdims=True)
        scalars = jnp.where(row_lane == COMPS + c, square, scalars)
    for f in range(MEMBERS):
        base = STRIDE * f
        for k in range(8):
            msg_ref[base + SHARE * k : base + SHARE * (k + 1), :] = tips[k][SHARE * f : SHARE * (f + 1), :]
        msg_ref[base + 8 * SHARE : base + 8 * SHARE + 1, :] = scalars


def pick(vector, k):
    return jnp.sum(jnp.where(lane_of((1, NY)) == k, vector, 0.0), axis=1, keepdims=True)


def total_of(block):
    return jnp.sum(jnp.sum(block, axis=0, keepdims=True), axis=1, keepdims=True)


def scalar_row(values):
    lane = lane_of((1, NY))
    row = jnp.zeros((1, NY), jnp.float32)
    for k, value in enumerate(values):
        row = jnp.where(lane == k, value, row)
    return row


def overlap(rate, count):
    shape = (8, NY)
    index = (row_of(shape) * NY + lane_of(shape) + 1).astype(jnp.float32)
    rho = total_of(jnp.where(index <= float(count), jnp.exp(-2.0 * rate * index), 0.0))
    omega = float(count) * jnp.exp(jnp.full((1, 1), -rate * float(count + 1), jnp.float32))
    return rho, omega


def other_half(x):
    return pltpu.roll(x, SHARE, 0)


def reach(rate, f, upper):
    steps = jnp.where(upper, float(f), float(MEMBERS - 1 - f))
    return jnp.exp(-rate * float(NX) * steps)


def group_kernel(member_ref, mine_ref, rate_ref, gain_ref, sigma_ref, got_ref, sums_ref, local_ref, msg_ref, pre_ref):
    rate, sigma = rate_ref[0], sigma_ref[0]
    gain4 = TAU * gain_ref[0]
    shape = (2 * SHARE, NY)
    upper = row_of(shape) < SHARE
    block = jnp.exp(jnp.full(shape, -rate * float(NX), jnp.float32))
    rho, omega = overlap(rate, NX)
    zero = jnp.zeros(shape, jnp.float32)

    def piece(f, k):
        start = STRIDE * f + 2 * SHARE * k
        return got_ref[start : start + 2 * SHARE, :]

    total = got_ref[STRIDE - 1 : STRIDE, :]
    for f in range(1, MEMBERS):
        total = total + got_ref[STRIDE * (f + 1) - 1 : STRIDE * (f + 1), :]
    sums = [pick(total, k) for k in range(2 * COMPS)]
    shifts = [sums[c] / (sums[COMPS + c] + EPS) + sigma for c in range(COMPS)]
    shift = jnp.where(member_ref[0] * SHARE < NZ, shifts[0], shifts[1])

    tips = [[piece(f, k) for f in range(MEMBERS)] for k in range(2)]
    ends, before = [], []
    for k in range(2):
        forward, backward = [zero], [zero]
        for f in range(MEMBERS):
            forward.append(block * forward[-1] + tips[k][f])
            backward.append(block * backward[-1] + tips[k][MEMBERS - 1 - f])
        ends.append(jnp.where(upper, forward[-1], backward[-1]))
        before.append([jnp.where(upper, forward[f], backward[MEMBERS - 1 - f]) for f in range(MEMBERS)])
    moment0, moment1, ww, wq, qq = (zero,) * 5
    for f in range(MEMBERS):
        pre_o, pre_a = gain4 * before[0][f], gain4 * before[1][f]
        pre_ref[4 * SHARE * f : 4 * SHARE * f + 2 * SHARE, :] = pre_o
        pre_ref[4 * SHARE * f + 2 * SHARE : 4 * SHARE * (f + 1), :] = pre_a
        own_q, own_p = piece(f, 2), piece(f, 3)
        weight = reach(rate, f, upper)
        spread_o = rho * pre_o + omega * other_half(pre_o)
        spread_a = rho * pre_a + omega * other_half(pre_a)
        moment0 = moment0 + weight * (own_p - spread_a)
        moment1 = moment1 + weight * (own_q + spread_o)
        y = pre_a - shift * pre_o
        spread_y = spread_a - shift * spread_o
        own_w = own_p + shift * own_q
        ww = ww + y * (spread_y - 2.0 * own_w)
        wq = wq + (pre_o * (own_w - spread_y) - y * own_q)
        qq = qq + pre_o * (2.0 * own_q + spread_o)
    values = list(sums)
    for c in range(COMPS):
        values += [jnp.sum(local_ref[3 * c + k : 3 * c + k + 1, :], axis=1, keepdims=True) for k in range(3)]
        values.append(local_shift(sums_ref, c, sigma))
    values += [total_of(ww), total_of(wq), total_of(qq), shift]
    scalars = scalar_row(values)
    for k in range(MEMBERS):
        for i, value in enumerate((gain4 * ends[0], gain4 * ends[1], moment1, moment0)):
            start = STRIDE * k + 2 * SHARE * i
            msg_ref[start : start + 2 * SHARE, :] = value
        msg_ref[STRIDE * (k + 1) - 1 : STRIDE * (k + 1), :] = scalars


def owner_kernel(groups, cells, member_ref, mine_ref, rate_ref, sigma_ref, got_ref, pre_ref, back_ref, mass_ref):
    rate, sigma = rate_ref[0], sigma_ref[0]
    member, mine = member_ref[0], mine_ref[0]
    shape = (2 * SHARE, NY)
    upper = row_of(shape) < SHARE
    span = NX * MEMBERS
    block = jnp.exp(jnp.full(shape, -rate * float(span), jnp.float32))
    wrap = 1.0 - jnp.exp(jnp.full(shape, -rate * float(span * groups), jnp.float32))
    rho, omega = overlap(rate, span)
    scal = got_ref[pl.ds(STRIDE - 1, 2 * groups, stride=STRIDE), :]
    lane = lane_of((2 * groups, NY))

    def column(k):
        return jnp.sum(jnp.where(lane == k, scal, 0.0), axis=1, keepdims=True)

    def expand(first, value):
        ww, wq, qq, base = [column(first + k) for k in range(4)]
        more = value - base
        return jnp.sum(ww + more * (2.0 * wq + more * qq), axis=0, keepdims=True)

    total = jnp.sum(scal, axis=0, keepdims=True)
    squares, shifts = [], []
    for c in range(COMPS):
        mean_square = pick(total, COMPS + c) / cells
        squares.append(mean_square)
        shifts.append((pick(total, c) / cells) / (mean_square + EPS) + sigma)
    mass_ref[...] = jnp.broadcast_to(scalar_row(squares + shifts), (8, NY))
    first = member * SHARE < NZ
    shift = jnp.where(first, shifts[0], shifts[1])

    def piece(g, y, k):
        start = STRIDE * (2 * g + y) + 2 * SHARE * k
        return got_ref[start : start + 2 * SHARE, :]

    zero = jnp.zeros(shape, jnp.float32)
    acc, chosen = zero, zero
    for y in range(2):
        ends = [piece(g, y, 1) - shift * piece(g, y, 0) for g in range(groups)]
        forward, backward = zero, zero
        for g in range(groups):
            forward = block * forward + ends[g]
            backward = block * backward + ends[groups - 1 - g]
        entering_f, entering_b = [forward / wrap], [backward / wrap]
        for g in range(groups - 1):
            entering_f.append(block * entering_f[-1] + ends[g])
            entering_b.append(block * entering_b[-1] + ends[groups - 1 - g])
        for g in range(groups):
            carry = jnp.where(upper, entering_f[g], entering_b[groups - 1 - g])
            moment = piece(g, y, 3) + shift * piece(g, y, 2)
            acc = acc + carry * (rho * carry + omega * other_half(carry) - 2.0 * moment)
            chosen = jnp.where(mine == 2 * g + y, carry, chosen)
    joined = total_of(acc) + expand(12, shift)
    values = []
    for c in range(COMPS):
        value = expand(4 + 4 * c, shifts[c])
        values.append(value + jnp.where(first == (c == 0), joined, 0.0))
    scalars = scalar_row(values)
    for f in range(MEMBERS):
        pre_o = pre_ref[4 * SHARE * f : 4 * SHARE * f + 2 * SHARE, :]
        pre_a = pre_ref[4 * SHARE * f + 2 * SHARE : 4 * SHARE * (f + 1), :]
        value = (pre_a - shift * pre_o) + reach(rate, f, upper) * chosen
        back_ref[BACK * f : BACK * f + 2 * SHARE, :] = value
        back_ref[BACK * (f + 1) - 1 : BACK * (f + 1), :] = scalars


def blend_kernel(mass_ref, p_hbm, q_hbm, w_ref, p_ref, q_ref, sems):
    size = NX * ROWS

    def fetch(k):
        block = pl.ds(k * size, size)
        return (
            pltpu.make_async_copy(p_hbm.at[block, :], p_ref.at[block, :], sems.at[0, k]),
            pltpu.make_async_copy(q_hbm.at[block, :], q_ref.at[block, :], sems.at[1, k]),
        )

    for k in range(LINES // ROWS):
        for one in fetch(k):
            one.start()
    for k in range(LINES // ROWS):
        comp = k * ROWS // NZ
        shift = jnp.broadcast_to(pick(mass_ref[0:1, :], COMPS + comp), (NX, NY))
        for one in fetch(k):
            one.wait()

        def step(i, _):
            place = pl.ds(pl.multiple_of(k * size + i * NX, NX), NX)
            w_ref[place, :] = p_ref[place, :] + shift * q_ref[place, :]
            return 0

        lax.fori_loop(0, ROWS, step, 0, unroll=2)


def finish_kernel(cells, rate_ref, got_ref, mass_ref, w_ref, out_hbm, out_scr, tab_scr, sems):
    blocks = LINES // ROWS
    size = NX * ROWS

    def copy(k):
        return pltpu.make_async_copy(out_scr.at[pl.ds(k * PITCH, NX), :], out_hbm.at[k], sems.at[k])

    rate = rate_ref[0]
    index = row_of((NX, NY)).astype(jnp.float32)
    tab_scr[0] = jnp.exp(-rate * (index + 1.0))
    tab_scr[1] = jnp.exp(-rate * (float(NX) - index))
    total = got_ref[BACK - 1 : BACK, :]
    for f in range(1, MEMBERS):
        total = total + got_ref[BACK * (f + 1) - 1 : BACK * (f + 1), :]
    scales = []
    for c in range(COMPS):
        mean_square = pick(mass_ref[0:1, :], c)
        ratio = jnp.sqrt(mean_square / (pick(total, c) / cells + EPS))
        scales.append(jnp.broadcast_to(ratio, (ROWS, NY)))

    def carries(k, half):
        members = range(k * ROWS // SHARE, (k + 1) * ROWS // SHARE)
        starts = [BACK * f + half * SHARE for f in members]
        return jnp.concatenate([got_ref[i : i + SHARE, :] for i in starts], axis=0)

    for k in range(blocks):
        comp = k * ROWS // NZ
        ratio = scales[comp]
        forward, backward = ratio * carries(k, 0), ratio * carries(k, 1)
        def step(x, _):
            rise = tab_scr[0, pl.ds(x, 1), :]
            fall = tab_scr[1, pl.ds(x, 1), :]
            place = pl.ds(pl.multiple_of(k * size + x * ROWS, ROWS), ROWS)
            value = ratio * w_ref[place, :]
            target = pl.ds(k * ROWS * PITCH + x, ROWS, stride=PITCH)
            out_scr[target, :] = value - (rise * forward + fall * backward)
            return 0

        lax.fori_loop(0, NX, step, 0, unroll=16)
        for line in range(ROWS):
            copy(k * ROWS + line).start()
    for line in range(LINES):
        copy(line).wait()


def far(x):
    return pltpu.with_memory_space_constraint(x, pltpu.HBM)


def near(x):
    return pltpu.with_memory_space_constraint(x, pltpu.VMEM)


def exchange(x, axes):
    peers = lax.axis_size(axes)
    moved = lax.all_to_all(x.reshape(peers, 1, x.size // peers), axes, 0, 0, tiled=True)
    return moved.reshape(x.shape)


def f32(*shape):
    return jax.ShapeDtypeStruct(shape, jnp.float32)


def shards(orbitals, potential, shift_ratio):
    groups = lax.axis_size(GX)
    devices = lax.axis_size(ALL)
    cells = float(NZ * NX * NY * devices)
    line_cells = NX * groups
    sigma = shift_ratio / float(line_cells * line_cells)
    rate = jnp.log1p(sigma + jnp.sqrt(sigma * (sigma + 2.0)))
    gain = jnp.sqrt(sigma / (sigma + 2.0))
    member = lax.axis_index(INNER).astype(jnp.int32)
    mine = lax.axis_index(OUTER).astype(jnp.int32)
    o = far(orbitals.reshape(LINES, NX, NY))
    cells_all = LINES * NX
    big = pltpu.VMEM((cells_all, NY), jnp.float32)
    distant = pltpu.HBM((cells_all, NY), jnp.float32)
    spread = pltpu.VMEM((LINES * PITCH, NY), jnp.float32)
    row = pltpu.VMEM((LINES, NY), jnp.float32)
    small = pltpu.VMEM((8, NY), jnp.float32)
    queue = pltpu.SemaphoreType.DMA((LINES,))

    o_near, v_near, edge, first, last = pl.pallas_call(
        load_kernel,
        out_shape=(spread, pltpu.VMEM((NZ * PITCH, NY), jnp.float32), row, row, row),
        in_specs=[HBM] * 2,
        out_specs=(VMEM,) * 5,
        scratch_shapes=[queue, pltpu.SemaphoreType.DMA((NZ,))],
        name="load",
        compiler_params=PARAMS,
    )(o, far(potential))
    halo = near(lax.ppermute(edge, "gy", [(0, 1), (1, 0)]))
    before = near(lax.ppermute(last, GX, [(i, (i + 1) % groups) for i in range(groups)]))
    o_near, edge, first = near(o_near), near(edge), near(first)

    a, tips, sums = pl.pallas_call(
        gather_kernel,
        out_shape=(big, pltpu.VMEM((8, LINES, NY), jnp.float32), small),
        in_specs=[SMEM, SMEM, SMEM, VMEM, VMEM],
        out_specs=(VMEM,) * 3,
        scratch_shapes=[pltpu.VMEM((4, NX, NY), jnp.float32)],
        name="gather",
        compiler_params=PARAMS,
    )(rate, gain, sigma, o_near, near(v_near))
    a, tips, sums = near(a), near(tips), near(sums)

    msg = pl.pallas_call(
        pack_kernel,
        out_shape=pltpu.VMEM((MEMBERS * STRIDE, NY), jnp.float32),
        in_specs=[SMEM, SMEM] + [VMEM] * 6,
        out_specs=VMEM,
        name="pack",
        compiler_params=PARAMS,
    )(rate, gain, tips, sums, edge, halo, first, before)
    got = exchange(msg, INNER)

    p, q, local = pl.pallas_call(
        sweep_kernel,
        out_shape=(distant, distant, small),
        in_specs=[SMEM] * 3 + [HBM] + [VMEM] * 4,
        out_specs=(HBM, HBM, VMEM),
        scratch_shapes=[big, big, spread]
        + [pltpu.VMEM((NX * NZ, NY), jnp.float32)] * 3
        + [queue, pltpu.SemaphoreType.DMA((2, COMPS))],
        name="sweep",
        compiler_params=PARAMS,
    )(rate, gain, sigma, o, a, edge, halo, sums)
    p, q, local = far(p), far(q), near(local)

    joint, pre = pl.pallas_call(
        group_kernel,
        out_shape=(
            pltpu.VMEM((MEMBERS * STRIDE, NY), jnp.float32),
            pltpu.VMEM((4 * SHARE * MEMBERS, NY), jnp.float32),
        ),
        in_specs=[SMEM] * 5 + [VMEM] * 3,
        out_specs=(VMEM,) * 2,
        name="group",
        compiler_params=PARAMS,
    )(member.reshape(1), mine.reshape(1), rate, gain, sigma, near(got), sums, local)
    outer = exchange(joint, OUTER)

    back, mass = pl.pallas_call(
        lambda *refs: owner_kernel(groups // MEMBERS, cells, *refs),
        out_shape=(pltpu.VMEM((MEMBERS * BACK, NY), jnp.float32), small),
        in_specs=[SMEM] * 4 + [VMEM] * 2,
        out_specs=(VMEM,) * 2,
        name="owner",
        compiler_params=PARAMS,
    )(member.reshape(1), mine.reshape(1), rate, sigma, near(outer), near(pre))
    returned = exchange(back, INNER)

    mass = near(mass)
    w = pl.pallas_call(
        blend_kernel,
        out_shape=big,
        in_specs=[VMEM, HBM, HBM],
        out_specs=VMEM,
        scratch_shapes=[big, big, pltpu.SemaphoreType.DMA((2, LINES // ROWS))],
        name="blend",
        compiler_params=PARAMS,
    )(mass, p, q)

    out = pl.pallas_call(
        lambda *refs: finish_kernel(cells, *refs),
        out_shape=f32(LINES, NX, NY),
        in_specs=[SMEM, VMEM, VMEM, VMEM],
        out_specs=HBM,
        scratch_shapes=[spread, pltpu.VMEM((2, NX, NY), jnp.float32), queue],
        name="finish",
        compiler_params=PARAMS,
    )(rate, near(returned), mass, near(w))
    return out.reshape(orbitals.shape)


def solution(mesh):
    split = Mesh(mesh.devices.reshape(2, 4, 8, 2, mesh.shape["gy"]), ALL)
    return jax.shard_map(
        shards,
        mesh=split,
        in_specs=(P(None, None, GX, "gy"), P(None, GX, "gy"), P()),
        out_specs=P(None, None, GX, "gy"),
        check_vma=False,
    )
```

```python
import jax
import jax.numpy as jnp
from jax import lax
from jax.experimental import pallas as pl
from jax.experimental.pallas import tpu as pltpu
from jax.sharding import Mesh
from jax.sharding import PartitionSpec as P

GX = ("gx_0", "gx_1", "gx_2", "gx_3")
INNER = ("gx_2", "gx_3")
OUTER = ("gx_0", "gx_1", "gy")
ALL = ("gx_0", "gx_1", "gx_2", "gx_3", "gy")

TAU = 4.0
EPS = 1e-06
COUPLING_FIRST = 0.06
COUPLING_SECOND = 0.05
COUPLING_CROSS = 0.04
HIGHEST = lax.Precision.HIGHEST

COMPS = 2
NZ = 32
NX = 64
NY = 128
LINES = COMPS * NZ
MEMBERS = 16
SHARE = LINES // MEMBERS
STRIDE = 8 * SHARE + 1
BACK = 2 * SHARE + 1
PITCH = NX + 8
ROWS = 8
UNROLL = 8

PARAMS = pltpu.CompilerParams(vmem_limit_bytes=16 << 20)
VMEM = pl.BlockSpec(memory_space=pltpu.VMEM)
HBM = pl.BlockSpec(memory_space=pltpu.HBM)
SMEM = pl.BlockSpec(memory_space=pltpu.SMEM)


def lane_of(shape):
    return lax.broadcasted_iota(jnp.int32, shape, 1)


def row_of(shape):
    return lax.broadcasted_iota(jnp.int32, shape, 0)


def rows(x, comp):
    return pl.ds(pl.multiple_of(x * LINES + comp * NZ, NZ), NZ)


def part(comp):
    return slice(comp * NZ, (comp + 1) * NZ)


def start_planes(source, target, sems):
    def copy(k):
        place = pl.ds(pl.multiple_of(k * PITCH, 8), NX)
        return pltpu.make_async_copy(source.at[k], target.at[place, :], sems.at[k])

    def start(k, _):
        copy(k).start()
        return 0

    lax.fori_loop(0, source.shape[0], start, 0, unroll=8)

    def wait(first, last):
        def one(k, _):
            copy(k).wait()
            return 0

        lax.fori_loop(first, last, one, 0, unroll=8)

    return wait


def line_rows(x, comp=0):
    return pl.ds(comp * NZ * PITCH + x, NZ, stride=PITCH)


def load_kernel(o_hbm, v_hbm, o_ref, v_ref, edge_ref, first_ref, last_ref, sems, v_sems):
    wait = start_planes(o_hbm, o_ref, sems)
    lane = lane_of((NZ, NY)) // 2
    for c in range(COMPS):
        wait(c * NZ, (c + 1) * NZ)
        if c == 0:
            wait_v = start_planes(v_hbm, v_ref, v_sems)

        def step(x, packed):
            return jnp.where(lane == x, pltpu.roll(o_ref[line_rows(x, c), :], 2 * x + 1, 1), packed)

        edge_ref[part(c), :] = lax.fori_loop(0, NX, step, jnp.zeros((NZ, NY), jnp.float32), unroll=16)
        first_ref[part(c), :] = o_ref[line_rows(0, c), :]
        last_ref[part(c), :] = o_ref[line_rows(NX - 1, c), :]
    wait_v(0, NZ)


def tables(rate, count):
    place = (row_of((count * NX, NY)) // count).astype(jnp.float32)
    index = row_of((NX, NY)).astype(jnp.float32)
    rise = jnp.exp(-rate * (index + 1.0))
    fall = jnp.exp(-rate * (float(NX) - index))
    shape = (count * NX, NX)
    gap = (row_of(shape) // count - lane_of(shape)).astype(jnp.float32)
    near = jnp.exp(-rate * jnp.abs(gap))
    return (
        jnp.exp(-rate * (float(NX - 1) - place)),
        jnp.exp(-rate * place),
        dot(near, rise),
        dot(near, fall),
    )


def gather_kernel(rate_ref, gain_ref, sigma_ref, o_ref, v_ref, a_ref, tips_ref, sums_ref, tab_scr):
    rate = rate_ref[0]
    gain4 = TAU * gain_ref[0]
    keep = 1.0 - TAU * sigma_ref[0]
    tip_f, tip_b, cell_r, cell_s = tables(rate, 1)
    tab_scr[0] = 0.5 * (tip_f + tip_b)
    tab_scr[1] = 0.5 * (tip_f - tip_b)
    tab_scr[2] = 0.5 * (cell_r + cell_s)
    tab_scr[3] = 0.5 * (cell_r - cell_s)
    zero = jnp.zeros((NZ, NY), jnp.float32)
    def fold(total, block):
        for b in range(NZ // ROWS):
            total = total + block[b * ROWS : (b + 1) * ROWS, :]
        return total

    def around_of(o):
        near_z = pltpu.roll(o, 1, 0) + pltpu.roll(o, NZ - 1, 0)
        return -0.5 * (near_z + (pltpu.roll(o, 1, 1) + pltpu.roll(o, NY - 1, 1)))

    def read(x):
        o = [o_ref[line_rows(x, c), :] for c in range(COMPS)]
        return o, [around_of(one) for one in o]

    def step(x, carry):
        before, o, around, cross, square = carry
        after = read(jnp.minimum(x + 1, NX - 1))
        s = [o[0] * o[0], o[1] * o[1]]
        both = COUPLING_CROSS * (s[0] + s[1])
        base = (v_ref[line_rows(x), :] + 2.0) + both
        own = (COUPLING_FIRST - COUPLING_CROSS, COUPLING_SECOND - COUPLING_CROSS)
        new_cross, new_square = [], []
        for c in range(COMPS):
            a = (base + own[c] * s[c]) * o[c] + around[c]
            a_ref[rows(x, c), :] = a
            new_cross.append(fold(cross[c], o[c] * ((a + o[c]) - before[c])))
            new_square.append(fold(square[c], s[c]))
        return o, after[0], after[1], new_cross, new_square

    part_sum = [jnp.zeros((ROWS, NY), jnp.float32)] * 2
    start = read(0)
    cross, square = lax.fori_loop(0, NX, step, ([zero] * 2, *start, part_sum, part_sum), unroll=UNROLL)[3:]

    sums = []
    for c in range(COMPS):
        def add(x, sums):
            y = NX - 1 - x
            weights = [tab_scr[k, pl.ds(x, 1), :] for k in range(4)]
            fields = (
                (o_ref[line_rows(x, c), :], o_ref[line_rows(y, c), :]),
                (a_ref[rows(x, c), :], a_ref[rows(y, c), :]),
            )
            return [
                [
                    old + weight * (one + two if k % 2 == 0 else one - two)
                    for k, (old, weight) in enumerate(zip(olds, weights))
                ]
                for olds, (one, two) in zip(sums, fields)
            ]

        found = lax.fori_loop(0, NX // 2, add, [[zero] * 4] * 2, unroll=4)
        sums.append([m for f in found for m in (f[0] + f[1], f[0] - f[1], f[2] + f[3], f[2] - f[3])])
    once = jnp.exp(jnp.full((NZ, NY), -rate, jnp.float32))
    for c in range(COMPS):
        f_o, b_o, r_o, s_o, f_a, b_a, r_a, s_a = sums[c]
        tips_ref[0, part(c), :] = f_o
        tips_ref[1, part(c), :] = b_o
        tips_ref[2, part(c), :] = f_a
        tips_ref[3, part(c), :] = b_a
        tips_ref[4, part(c), :] = gain4 * r_o
        tips_ref[5, part(c), :] = gain4 * s_o
        tips_ref[6, part(c), :] = keep * (once * b_o) - gain4 * r_a
        tips_ref[7, part(c), :] = keep * (once * f_o) - gain4 * s_a
        sums_ref[c : c + 1, :] = jnp.sum(cross[c], axis=0, keepdims=True)
        sums_ref[COMPS + c : COMPS + c + 1, :] = jnp.sum(square[c], axis=0, keepdims=True)


def local_shift(sums_ref, c, sigma):
    cross = jnp.sum(sums_ref[c : c + 1, :], axis=1, keepdims=True)
    square = jnp.sum(sums_ref[COMPS + c : COMPS + c + 1, :], axis=1, keepdims=True)
    return cross / (square + EPS) + sigma


def sweep_kernel(rate_ref, gain_ref, sigma_ref, o_hbm, a_ref, edge_ref, halo_ref, sums_ref, p_hbm, q_hbm, local_ref, p_ref, q_ref, o_ref, fo_scr, fa_scr, a_scr, sems, out_sems):
    wait = start_planes(o_hbm, o_ref, sems)

    def send(c):
        block = pl.ds(c * NZ * NX, NZ * NX)
        return (
            pltpu.make_async_copy(p_ref.at[block, :], p_hbm.at[block, :], out_sems.at[0, c]),
            pltpu.make_async_copy(q_ref.at[block, :], q_hbm.at[block, :], out_sems.at[1, c]),
        )

    gain4 = TAU * gain_ref[0]
    keep = 1.0 - TAU * sigma_ref[0]
    decay = jnp.exp(jnp.full((NZ, NY), -rate_ref[0], jnp.float32))
    lane = lane_of((NZ, NY))
    zero = jnp.zeros((NZ, NY), jnp.float32)
    lane1 = lane_of((1, NY))
    for c in range(COMPS):
        delta = -0.5 * (halo_ref[part(c), :] - edge_ref[part(c), :])
        even = lane % 2 == 0
        delta = jnp.where(even, pltpu.roll(delta, NY - 1, 1), pltpu.roll(delta, 1, 1))
        ends = (lane == 0) | (lane == NY - 1)

        def ahead(x, carry):
            fo, fa = carry
            o = o_ref[line_rows(x, c), :]
            a = a_ref[rows(x, c), :] + jnp.where(ends, pltpu.roll(delta, NY - (2 * x + 1), 1), 0.0)
            fo = decay * fo + o
            fa = decay * fa + a
            fo_scr[pl.ds(pl.multiple_of(x * NZ, NZ), NZ), :] = fo
            fa_scr[pl.ds(pl.multiple_of(x * NZ, NZ), NZ), :] = fa
            a_scr[pl.ds(pl.multiple_of(x * NZ, NZ), NZ), :] = a
            return fo, fa

        wait(c * NZ, (c + 1) * NZ)
        lax.fori_loop(0, NX, ahead, (zero, zero), unroll=8)
        shift = jnp.broadcast_to(local_shift(sums_ref, c, sigma_ref[0]), (NZ, NY))

        def behind(k, carry):
            x = NX - 1 - k
            bo, ba, ww, wq, qq = carry
            o, a = o_ref[line_rows(x, c), :], a_scr[pl.ds(pl.multiple_of(x * NZ, NZ), NZ), :]
            do, da = decay * bo, decay * ba
            q = gain4 * (fo_scr[pl.ds(pl.multiple_of(x * NZ, NZ), NZ), :] + do)
            p = keep * o - gain4 * (fa_scr[pl.ds(pl.multiple_of(x * NZ, NZ), NZ), :] + da)
            for b in range(NZ // ROWS):
                place = pl.ds(pl.multiple_of(((c * NZ // ROWS + b) * NX + x) * ROWS, ROWS), ROWS)
                q_ref[place, :] = q[b * ROWS : (b + 1) * ROWS, :]
                p_ref[place, :] = p[b * ROWS : (b + 1) * ROWS, :]
            w = p + shift * q
            return do + o, da + a, ww + w * w, wq + w * q, qq + q * q

        _, _, ww, wq, qq = lax.fori_loop(0, NX, behind, (zero,) * 5, unroll=8)
        for k, value in enumerate((ww, wq, qq)):
            local_ref[3 * c + k : 3 * c + k + 1, :] = jnp.sum(value, axis=0, keepdims=True)
        for one in send(c):
            one.start()
    for c in range(COMPS):
        for one in send(c):
            one.wait()


def dot(a, b):
    return jnp.dot(a, b, precision=HIGHEST, preferred_element_type=jnp.float32)


def pack_kernel(rate_ref, gain_ref, tips_ref, sums_ref, edge_ref, halo_ref, first_ref, before_ref, msg_ref):
    gain4 = TAU * gain_ref[0]
    halo = halo_ref[...]
    delta = -0.5 * (halo - edge_ref[...])
    shape = (NY, NY)
    odd = row_of(shape) % 2
    hit = ((lane_of(shape) == 0) & (odd == 0)) | ((lane_of(shape) == NY - 1) & (odd == 1))
    fixes = [dot(delta, jnp.where(hit, table, 0.0)) for table in tables(rate_ref[0], 2)]
    tips = [tips_ref[k] for k in range(8)]
    tips[2] = tips[2] + fixes[0]
    tips[3] = tips[3] + fixes[1]
    tips[6] = tips[6] - gain4 * fixes[2]
    tips[7] = tips[7] - gain4 * fixes[3]

    lane = lane_of((LINES, NY))
    even = lane % 2 == 0
    swapped = jnp.where(even, pltpu.roll(delta, NY - 1, 1), pltpu.roll(delta, 1, 1))
    extra = edge_ref[...] * swapped - first_ref[...] * before_ref[...]
    row_lane = lane_of((1, NY))
    scalars = jnp.zeros((1, NY), jnp.float32)
    for c in range(COMPS):
        cross = sums_ref[c : c + 1, :] + jnp.sum(extra[c * NZ : (c + 1) * NZ, :], axis=0, keepdims=True)
        scalars = jnp.where(row_lane == c, jnp.sum(cross, axis=1, keepdims=True), scalars)
        square = jnp.sum(sums_ref[COMPS + c : COMPS + c + 1, :], axis=1, keepdims=True)
        scalars = jnp.where(row_lane == COMPS + c, square, scalars)
    for f in range(MEMBERS):
        base = STRIDE * f
        for k in range(8):
            msg_ref[base + SHARE * k : base + SHARE * (k + 1), :] = tips[k][SHARE * f : SHARE * (f + 1), :]
        msg_ref[base + 8 * SHARE : base + 8 * SHARE + 1, :] = scalars


def pick(vector, k):
    return jnp.sum(jnp.where(lane_of((1, NY)) == k, vector, 0.0), axis=1, keepdims=True)


def total_of(block):
    return jnp.sum(jnp.sum(block, axis=0, keepdims=True), axis=1, keepdims=True)


def scalar_row(values):
    lane = lane_of((1, NY))
    row = jnp.zeros((1, NY), jnp.float32)
    for k, value in enumerate(values):
        row = jnp.where(lane == k, value, row)
    return row


def overlap(rate, count):
    shape = (8, NY)
    index = (row_of(shape) * NY + lane_of(shape) + 1).astype(jnp.float32)
    rho = total_of(jnp.where(index <= float(count), jnp.exp(-2.0 * rate * index), 0.0))
    omega = float(count) * jnp.exp(jnp.full((1, 1), -rate * float(count + 1), jnp.float32))
    return rho, omega


def other_half(x):
    return pltpu.roll(x, SHARE, 0)


def reach(rate, f, upper):
    steps = jnp.where(upper, float(f), float(MEMBERS - 1 - f))
    return jnp.exp(-rate * float(NX) * steps)


def group_kernel(member_ref, mine_ref, rate_ref, gain_ref, sigma_ref, got_ref, sums_ref, local_ref, msg_ref, pre_ref):
    rate, sigma = rate_ref[0], sigma_ref[0]
    gain4 = TAU * gain_ref[0]
    shape = (2 * SHARE, NY)
    upper = row_of(shape) < SHARE
    block = jnp.exp(jnp.full(shape, -rate * float(NX), jnp.float32))
    rho, omega = overlap(rate, NX)
    zero = jnp.zeros(shape, jnp.float32)

    def piece(f, k):
        start = STRIDE * f + 2 * SHARE * k
        return got_ref[start : start + 2 * SHARE, :]

    total = got_ref[STRIDE - 1 : STRIDE, :]
    for f in range(1, MEMBERS):
        total = total + got_ref[STRIDE * (f + 1) - 1 : STRIDE * (f + 1), :]
    sums = [pick(total, k) for k in range(2 * COMPS)]
    shifts = [sums[c] / (sums[COMPS + c] + EPS) + sigma for c in range(COMPS)]
    shift = jnp.where(member_ref[0] * SHARE < NZ, shifts[0], shifts[1])

    tips = [[piece(f, k) for f in range(MEMBERS)] for k in range(2)]
    ends, before = [], []
    for k in range(2):
        forward, backward = [zero], [zero]
        for f in range(MEMBERS):
            forward.append(block * forward[-1] + tips[k][f])
            backward.append(block * backward[-1] + tips[k][MEMBERS - 1 - f])
        ends.append(jnp.where(upper, forward[-1], backward[-1]))
        before.append([jnp.where(upper, forward[f], backward[MEMBERS - 1 - f]) for f in range(MEMBERS)])
    moment0, moment1, ww, wq, qq = (zero,) * 5
    for f in range(MEMBERS):
        pre_o, pre_a = gain4 * before[0][f], gain4 * before[1][f]
        pre_ref[4 * SHARE * f : 4 * SHARE * f + 2 * SHARE, :] = pre_o
        pre_ref[4 * SHARE * f + 2 * SHARE : 4 * SHARE * (f + 1), :] = pre_a
        own_q, own_p = piece(f, 2), piece(f, 3)
        weight = reach(rate, f, upper)
        spread_o = rho * pre_o + omega * other_half(pre_o)
        spread_a = rho * pre_a + omega * other_half(pre_a)
        moment0 = moment0 + weight * (own_p - spread_a)
        moment1 = moment1 + weight * (own_q + spread_o)
        y = pre_a - shift * pre_o
        spread_y = spread_a - shift * spread_o
        own_w = own_p + shift * own_q
        ww = ww + y * (spread_y - 2.0 * own_w)
        wq = wq + (pre_o * (own_w - spread_y) - y * own_q)
        qq = qq + pre_o * (2.0 * own_q + spread_o)
    values = list(sums)
    for c in range(COMPS):
        values += [jnp.sum(local_ref[3 * c + k : 3 * c + k + 1, :], axis=1, keepdims=True) for k in range(3)]
        values.append(local_shift(sums_ref, c, sigma))
    values += [total_of(ww), total_of(wq), total_of(qq), shift]
    scalars = scalar_row(values)
    for k in range(MEMBERS):
        for i, value in enumerate((gain4 * ends[0], gain4 * ends[1], moment1, moment0)):
            start = STRIDE * k + 2 * SHARE * i
            msg_ref[start : start + 2 * SHARE, :] = value
        msg_ref[STRIDE * (k + 1) - 1 : STRIDE * (k + 1), :] = scalars


def owner_kernel(groups, cells, member_ref, mine_ref, rate_ref, sigma_ref, got_ref, pre_ref, back_ref, mass_ref):
    rate, sigma = rate_ref[0], sigma_ref[0]
    member, mine = member_ref[0], mine_ref[0]
    shape = (2 * SHARE, NY)
    upper = row_of(shape) < SHARE
    span = NX * MEMBERS
    block = jnp.exp(jnp.full(shape, -rate * float(span), jnp.float32))
    wrap = 1.0 - jnp.exp(jnp.full(shape, -rate * float(span * groups), jnp.float32))
    rho, omega = overlap(rate, span)
    scal = got_ref[pl.ds(STRIDE - 1, 2 * groups, stride=STRIDE), :]
    lane = lane_of((2 * groups, NY))

    def column(k):
        return jnp.sum(jnp.where(lane == k, scal, 0.0), axis=1, keepdims=True)

    def expand(first, value):
        ww, wq, qq, base = [column(first + k) for k in range(4)]
        more = value - base
        return jnp.sum(ww + more * (2.0 * wq + more * qq), axis=0, keepdims=True)

    total = jnp.sum(scal, axis=0, keepdims=True)
    squares, shifts = [], []
    for c in range(COMPS):
        mean_square = pick(total, COMPS + c) / cells
        squares.append(mean_square)
        shifts.append((pick(total, c) / cells) / (mean_square + EPS) + sigma)
    mass_ref[...] = jnp.broadcast_to(scalar_row(squares + shifts), (8, NY))
    first = member * SHARE < NZ
    shift = jnp.where(first, shifts[0], shifts[1])

    def piece(g, y, k):
        start = STRIDE * (2 * g + y) + 2 * SHARE * k
        return got_ref[start : start + 2 * SHARE, :]

    zero = jnp.zeros(shape, jnp.float32)
    acc, chosen = zero, zero
    for y in range(2):
        ends = [piece(g, y, 1) - shift * piece(g, y, 0) for g in range(groups)]
        forward, backward = zero, zero
        for g in range(groups):
            forward = block * forward + ends[g]
            backward = block * backward + ends[groups - 1 - g]
        entering_f, entering_b = [forward / wrap], [backward / wrap]
        for g in range(groups - 1):
            entering_f.append(block * entering_f[-1] + ends[g])
            entering_b.append(block * entering_b[-1] + ends[groups - 1 - g])
        for g in range(groups):
            carry = jnp.where(upper, entering_f[g], entering_b[groups - 1 - g])
            moment = piece(g, y, 3) + shift * piece(g, y, 2)
            acc = acc + carry * (rho * carry + omega * other_half(carry) - 2.0 * moment)
            chosen = jnp.where(mine == 2 * g + y, carry, chosen)
    joined = total_of(acc) + expand(12, shift)
    values = []
    for c in range(COMPS):
        value = expand(4 + 4 * c, shifts[c])
        values.append(value + jnp.where(first == (c == 0), joined, 0.0))
    scalars = scalar_row(values)
    for f in range(MEMBERS):
        pre_o = pre_ref[4 * SHARE * f : 4 * SHARE * f + 2 * SHARE, :]
        pre_a = pre_ref[4 * SHARE * f + 2 * SHARE : 4 * SHARE * (f + 1), :]
        value = (pre_a - shift * pre_o) + reach(rate, f, upper) * chosen
        back_ref[BACK * f : BACK * f + 2 * SHARE, :] = value
        back_ref[BACK * (f + 1) - 1 : BACK * (f + 1), :] = scalars


def blend_kernel(mass_ref, p_hbm, q_hbm, w_ref, p_ref, q_ref, sems):
    size = NX * ROWS

    def fetch(k):
        block = pl.ds(k * size, size)
        return (
            pltpu.make_async_copy(p_hbm.at[block, :], p_ref.at[block, :], sems.at[0, k]),
            pltpu.make_async_copy(q_hbm.at[block, :], q_ref.at[block, :], sems.at[1, k]),
        )

    for k in range(LINES // ROWS):
        for one in fetch(k):
            one.start()
    for k in range(LINES // ROWS):
        comp = k * ROWS // NZ
        shift = jnp.broadcast_to(pick(mass_ref[0:1, :], COMPS + comp), (NX, NY))
        for one in fetch(k):
            one.wait()

        def step(i, _):
            place = pl.ds(pl.multiple_of(k * size + i * NX, NX), NX)
            w_ref[place, :] = p_ref[place, :] + shift * q_ref[place, :]
            return 0

        lax.fori_loop(0, ROWS, step, 0, unroll=2)


def finish_kernel(cells, rate_ref, got_ref, mass_ref, w_ref, out_hbm, out_scr, tab_scr, sems):
    blocks = LINES // ROWS
    size = NX * ROWS

    def copy(k):
        return pltpu.make_async_copy(out_scr.at[pl.ds(k * PITCH, NX), :], out_hbm.at[k], sems.at[k])

    rate = rate_ref[0]
    index = row_of((NX, NY)).astype(jnp.float32)
    tab_scr[0] = jnp.exp(-rate * (index + 1.0))
    tab_scr[1] = jnp.exp(-rate * (float(NX) - index))
    total = got_ref[BACK - 1 : BACK, :]
    for f in range(1, MEMBERS):
        total = total + got_ref[BACK * (f + 1) - 1 : BACK * (f + 1), :]
    scales = []
    for c in range(COMPS):
        mean_square = pick(mass_ref[0:1, :], c)
        ratio = jnp.sqrt(mean_square / (pick(total, c) / cells + EPS))
        scales.append(jnp.broadcast_to(ratio, (ROWS, NY)))

    def carries(k, half):
        members = range(k * ROWS // SHARE, (k + 1) * ROWS // SHARE)
        starts = [BACK * f + half * SHARE for f in members]
        return jnp.concatenate([got_ref[i : i + SHARE, :] for i in starts], axis=0)

    for k in range(blocks):
        comp = k * ROWS // NZ
        ratio = scales[comp]
        forward, backward = ratio * carries(k, 0), ratio * carries(k, 1)
        def step(x, _):
            rise = tab_scr[0, pl.ds(x, 1), :]
            fall = tab_scr[1, pl.ds(x, 1), :]
            place = pl.ds(pl.multiple_of(k * size + x * ROWS, ROWS), ROWS)
            value = ratio * w_ref[place, :]
            target = pl.ds(k * ROWS * PITCH + x, ROWS, stride=PITCH)
            out_scr[target, :] = value - (rise * forward + fall * backward)
            return 0

        lax.fori_loop(0, NX, step, 0, unroll=16)
        for line in range(ROWS):
            copy(k * ROWS + line).start()
    for line in range(LINES):
        copy(line).wait()


def far(x):
    return pltpu.with_memory_space_constraint(x, pltpu.HBM)


def near(x):
    return pltpu.with_memory_space_constraint(x, pltpu.VMEM)


def exchange(x, axes):
    peers = lax.axis_size(axes)
    moved = lax.all_to_all(x.reshape(peers, 1, x.size // peers), axes, 0, 0, tiled=True)
    return moved.reshape(x.shape)


def f32(*shape):
    return jax.ShapeDtypeStruct(shape, jnp.float32)


def shards(orbitals, potential, shift_ratio):
    groups = lax.axis_size(GX)
    devices = lax.axis_size(ALL)
    cells = float(NZ * NX * NY * devices)
    line_cells = NX * groups
    sigma = shift_ratio / float(line_cells * line_cells)
    rate = jnp.log1p(sigma + jnp.sqrt(sigma * (sigma + 2.0)))
    gain = jnp.sqrt(sigma / (sigma + 2.0))
    member = lax.axis_index(INNER).astype(jnp.int32)
    mine = lax.axis_index(OUTER).astype(jnp.int32)
    o = far(orbitals.reshape(LINES, NX, NY))
    cells_all = LINES * NX
    big = pltpu.VMEM((cells_all, NY), jnp.float32)
    distant = pltpu.HBM((cells_all, NY), jnp.float32)
    spread = pltpu.VMEM((LINES * PITCH, NY), jnp.float32)
    row = pltpu.VMEM((LINES, NY), jnp.float32)
    small = pltpu.VMEM((8, NY), jnp.float32)
    queue = pltpu.SemaphoreType.DMA((LINES,))

    o_near, v_near, edge, first, last = pl.pallas_call(
        load_kernel,
        out_shape=(spread, pltpu.VMEM((NZ * PITCH, NY), jnp.float32), row, row, row),
        in_specs=[HBM] * 2,
        out_specs=(VMEM,) * 5,
        scratch_shapes=[queue, pltpu.SemaphoreType.DMA((NZ,))],
        name="load",
        compiler_params=PARAMS,
    )(o, far(potential))
    halo = near(lax.ppermute(edge, "gy", [(0, 1), (1, 0)]))
    before = near(lax.ppermute(last, GX, [(i, (i + 1) % groups) for i in range(groups)]))
    o_near, edge, first = near(o_near), near(edge), near(first)

    a, tips, sums = pl.pallas_call(
        gather_kernel,
        out_shape=(big, pltpu.VMEM((8, LINES, NY), jnp.float32), small),
        in_specs=[SMEM, SMEM, SMEM, VMEM, VMEM],
        out_specs=(VMEM,) * 3,
        scratch_shapes=[pltpu.VMEM((4, NX, NY), jnp.float32)],
        name="gather",
        compiler_params=PARAMS,
    )(rate, gain, sigma, o_near, near(v_near))
    a, tips, sums = near(a), near(tips), near(sums)

    msg = pl.pallas_call(
        pack_kernel,
        out_shape=pltpu.VMEM((MEMBERS * STRIDE, NY), jnp.float32),
        in_specs=[SMEM, SMEM] + [VMEM] * 6,
        out_specs=VMEM,
        name="pack",
        compiler_params=PARAMS,
    )(rate, gain, tips, sums, edge, halo, first, before)
    got = exchange(msg, INNER)

    p, q, local = pl.pallas_call(
        sweep_kernel,
        out_shape=(distant, distant, small),
        in_specs=[SMEM] * 3 + [HBM] + [VMEM] * 4,
        out_specs=(HBM, HBM, VMEM),
        scratch_shapes=[big, big, spread]
        + [pltpu.VMEM((NX * NZ, NY), jnp.float32)] * 3
        + [queue, pltpu.SemaphoreType.DMA((2, COMPS))],
        name="sweep",
        compiler_params=PARAMS,
    )(rate, gain, sigma, o, a, edge, halo, sums)
    p, q, local = far(p), far(q), near(local)

    joint, pre = pl.pallas_call(
        group_kernel,
        out_shape=(
            pltpu.VMEM((MEMBERS * STRIDE, NY), jnp.float32),
            pltpu.VMEM((4 * SHARE * MEMBERS, NY), jnp.float32),
        ),
        in_specs=[SMEM] * 5 + [VMEM] * 3,
        out_specs=(VMEM,) * 2,
        name="group",
        compiler_params=PARAMS,
    )(member.reshape(1), mine.reshape(1), rate, gain, sigma, near(got), sums, local)
    outer = exchange(joint, OUTER)

    back, mass = pl.pallas_call(
        lambda *refs: owner_kernel(groups // MEMBERS, cells, *refs),
        out_shape=(pltpu.VMEM((MEMBERS * BACK, NY), jnp.float32), small),
        in_specs=[SMEM] * 4 + [VMEM] * 2,
        out_specs=(VMEM,) * 2,
        name="owner",
        compiler_params=PARAMS,
    )(member.reshape(1), mine.reshape(1), rate, sigma, near(outer), near(pre))
    returned = exchange(back, INNER)

    mass = near(mass)
    w = pl.pallas_call(
        blend_kernel,
        out_shape=big,
        in_specs=[VMEM, HBM, HBM],
        out_specs=VMEM,
        scratch_shapes=[big, big, pltpu.SemaphoreType.DMA((2, LINES // ROWS))],
        name="blend",
        compiler_params=PARAMS,
    )(mass, p, q)

    out = pl.pallas_call(
        lambda *refs: finish_kernel(cells, *refs),
        out_shape=f32(LINES, NX, NY),
        in_specs=[SMEM, VMEM, VMEM, VMEM],
        out_specs=HBM,
        scratch_shapes=[spread, pltpu.VMEM((2, NX, NY), jnp.float32), queue],
        name="finish",
        compiler_params=PARAMS,
    )(rate, near(returned), mass, near(w))
    return out.reshape(orbitals.shape)


def solution(mesh):
    split = Mesh(mesh.devices.reshape(2, 4, 8, 2, mesh.shape["gy"]), ALL)
    return jax.shard_map(
        shards,
        mesh=split,
        in_specs=(P(None, None, GX, "gy"), P(None, GX, "gy"), P()),
        out_specs=P(None, None, GX, "gy"),
        check_vma=False,
    )
```
